32 devices in a mesh: spatial: 8 (over z, x), filter: 4 (over y, core).
Axes of the slice: x: 2, y: 2, z: 4, core: 2. Of those that a mesh axis runs over, the one named last changes fastest.
Arguments:
- volume_in: bfloat16 [128, 32, 8192], P('filter', 'spatial'), may hold values from -6 to 6
- filters_a: bfloat16 [27, 256, 128], P(None, 'filter'), may hold values from -0.109375 to 0.109375
- bias_a: bfloat16 [256], P('filter'), may hold values from -0.5 to 0.5
- filters_b: bfloat16 [27, 256, 256], P(None, 'filter'), may hold values from -0.078125 to 0.078125
- bias_b: bfloat16 [256], P('filter'), may hold values from -0.5 to 0.5
Outputs:
- volume_out: bfloat16 [256, 8, 512], P('filter', 'spatial')
The draws below stay inside these ranges and needn't reach their ends.
All inputs are finite; a program needn't handle non-finite values.
Results may differ from the reference program's by a relative error of at most 0.0048.
Values may be sent and summed in bfloat16 or wider, within the bound.
A program may use at most 128 MiB of HBM per device.

```python
import jax
import jax.numpy as jnp
from jax import lax

C_IN = 128
C_MID = 256
ROWS = 64
COLS = 128
DEPTH = 32


def block_levels(rng, extent, shards, least, largest):
    loudness, own = 1.0, jax.random.fold_in(rng, 6)
    for position, shards_of in shards:
        heights = jnp.exp(jax.random.uniform(jax.random.fold_in(own, position), (shards_of,), jnp.float32, least / len(shards), largest / len(shards)))
        loudness = loudness * jnp.repeat(heights, extent[position] // shards_of).reshape([-1 if axis == position else 1 for axis in range(len(extent))])
    return loudness


def gaussian(rng, dims, scale, bound, pieces=(), dtype=jnp.bfloat16):
    array = scale * jax.random.normal(rng, dims, jnp.float32)
    if pieces:
        array = array * block_levels(rng, dims, pieces, -0.22, 0.18)
    return jnp.clip(array, -bound, bound).astype(dtype)


def setup_inputs(seed: int = 0) -> dict:
    key_of = jax.random.split(jax.random.key(seed), 6)
    volume_in = gaussian(key_of[0], (C_IN, DEPTH, ROWS * COLS), 1.0, 6.0, ((0, 4), (1, 8)))
    filters_a = gaussian(key_of[1], (27, C_MID, C_IN), (27 * C_IN) ** -0.5, 0.109375, ((1, 4),))
    bias_a = jnp.clip(jax.random.uniform(key_of[2], (C_MID,), jnp.float32, -0.5, 0.5) * block_levels(key_of[2], (C_MID,), ((0, 4),), -0.4, 0.0), -0.5, 0.5).astype(jnp.bfloat16)
    filters_b = gaussian(key_of[3], (27, C_MID, C_MID), (27 * C_MID) ** -0.5, 0.078125, ((1, 4),))
    bias_b = jnp.clip(jax.random.uniform(key_of[4], (C_MID,), jnp.float32, -0.5, 0.5) * block_levels(key_of[4], (C_MID,), ((0, 4),), -0.4, 0.0), -0.5, 0.5).astype(jnp.bfloat16)
    return dict(volume_in=volume_in, filters_a=filters_a, bias_a=bias_a, filters_b=filters_b, bias_b=bias_b)


def stride_layer(inputs, weight, bias_vec, slices, row_count, col_count):
    channels = inputs.shape[0]
    outputs = weight.shape[1]
    volume = inputs.reshape(1, channels, slices, row_count, col_count)
    kernel = weight.reshape(3, 3, 3, outputs, channels)
    summed = lax.conv_general_dilated(volume, kernel, (2, 2, 2), ((1, 1), (1, 1), (1, 1)), dimension_numbers=("NCDHW", "DHWOI", "NCDHW"), preferred_element_type=jnp.float32)[0]
    summed = summed + bias_vec.astype(jnp.float32)[:, None, None, None]
    active = jnp.where(summed > 0, summed, 0.2 * summed)
    return active.astype(jnp.bfloat16).reshape(outputs, slices // 2, (row_count // 2) * (col_count // 2))


def reference(volume_in, filters_a, bias_a, filters_b, bias_b):
    hidden = stride_layer(volume_in, filters_a, bias_a, DEPTH, ROWS, COLS)
    return stride_layer(hidden, filters_b, bias_b, DEPTH // 2, ROWS // 2, COLS // 2)
```

```python
import jax
import jax.numpy as jnp
import numpy as np
from jax import lax
from jax.experimental import pallas as pl
from jax.experimental.pallas import tpu as pltpu
from jax.sharding import PartitionSpec as P

MESH = pl.DeviceIdType.MESH
ROWS = 64
COLS = 128
F32 = jnp.float32
BF16 = jnp.bfloat16


def shifted(block, axis, distance):
    devices = range(lax.axis_size(axis))
    route = [(i - distance, i) for i in devices if i - distance in devices]
    return lax.ppermute(block, axis, route)


def local_conv(block, weight, pad_rows, row_count, col_count):
    channels = block.shape[0]
    slices = block.shape[1]
    volume = block.reshape(1, channels, slices, row_count, col_count)
    kernel = weight.reshape(3, 3, 3, weight.shape[1], weight.shape[2])
    return lax.conv_general_dilated(
        volume,
        kernel,
        (2, 2, 2),
        ((0, 0), (pad_rows, pad_rows), (1, 1)),
        dimension_numbers=("NCDHW", "DHWOI", "NCDHW"),
        preferred_element_type=F32,
    )[0]


def activate(summed, bias_vec):
    summed = summed + bias_vec.astype(F32)[:, None, None, None]
    return jnp.where(summed > 0, summed, 0.2 * summed).astype(BF16)


def gathered(volume_in, filters_a, bias_a, filters_b, bias_b):
    slices = volume_in.shape[1]
    outputs = filters_a.shape[1]
    extended = jnp.concatenate([shifted(volume_in[:, -1:], "spatial", 1), volume_in], 1)
    full = lax.all_gather(extended, "filter", axis=0, tiled=True)
    hidden = activate(local_conv(full, filters_a, 1, ROWS, COLS), bias_a)
    hidden = hidden.reshape(outputs, slices // 2, ROWS // 2 * (COLS // 2))
    extended = jnp.concatenate([shifted(hidden[:, -1:], "spatial", 1), hidden], 1)
    full = lax.all_gather(extended, "filter", axis=0, tiled=True)
    out = activate(local_conv(full, filters_b, 1, ROWS // 2, COLS // 2), bias_b)
    return out.reshape(filters_b.shape[1], slices // 4, ROWS // 4 * (COLS // 4))


HALF = 2048
QUARTER = 512


def pick_first():
    s = np.zeros((256, 3, 128), np.float32)
    for l in range(3):
        for row in range(2):
            for w in range(64):
                source = 2 * w + l - 1
                if source >= 0:
                    s[row * 128 + source, l, row * 64 + w] = 1
    return s.reshape(256, 384)


def pick_second():
    s = np.zeros((2, 512, 3, 128), np.float32)
    for half in range(2):
        for l in range(3):
            for row in range(4):
                for w in range(32):
                    source = 2 * w + l - 1
                    if source >= 0:
                        s[half, row * 128 + half * 64 + source, l, row * 32 + w] = 1
    return s.reshape(2, 512, 384)


def column(row_ref):
    row = lax.broadcasted_iota(jnp.int32, (64, 64), 0)
    col = lax.broadcasted_iota(jnp.int32, (64, 64), 1)
    spread = jnp.broadcast_to(row_ref[...].astype(F32), (64, 64))
    diagonal = jnp.where(row == col, spread, 0.0).astype(BF16)
    return jnp.dot(diagonal, jnp.ones((64, 256), BF16), preferred_element_type=F32)


def leaky(u):
    return jnp.where(u > 0, u, 0.2 * u).astype(BF16)


def kernel(
    n_spatial, xin, fa_in, fb_in, ba_in, bb_in, s1_in, s2_in, out,
    fa, ba, bb, fb, s1, s2, xv, x, xh, wa_send, wa, wb_send, wb, v0, v1, part, sib, y_send, y_recv, hid, v2,
    part2, sib2, z_send, z_recv,
    in_sems, x_sem, halo_sems, wa_sems, wb_sems, sib_sems, y_sems, hid_sems, sib2_sems, z_sems,
):
    s = lax.axis_index("spatial")
    f = lax.axis_index("filter")
    core, chip = f % 2, f // 2
    sibling = chip * 2 + (1 - core)
    partner = (1 - chip) * 2 + core
    diagonal = (1 - chip) * 2 + (1 - core)
    slot = core * 2 + chip
    peers = (diagonal, partner, sibling)
    is_first, is_last = s == 0, s == n_spatial - 1
    half = (s // 2) % 2
    mate = s + 2 - 4 * half

    load_fa = pltpu.make_async_copy(fa_in, fa, in_sems.at[3])
    load_fa.start()
    load = pltpu.make_async_copy(xin, xv, x_sem)
    load.start()
    load_fb = pltpu.make_async_copy(fb_in, fb, in_sems.at[0])
    load_s1 = pltpu.make_async_copy(s1_in, s1, in_sems.at[1])
    load_s2 = pltpu.make_async_copy(s2_in, s2, in_sems.at[2])
    load_fb.start()
    load_s1.start()
    load_s2.start()
    load_ba = pltpu.make_async_copy(ba_in, ba, in_sems.at[4])
    load_bb = pltpu.make_async_copy(bb_in, bb, in_sems.at[5])
    load_ba.start()
    load_bb.start()
    barrier = pltpu.get_barrier_semaphore()
    for peer in peers:
        pl.semaphore_signal(barrier, inc=1, device_id=(s, peer), device_id_type=MESH)
    pl.semaphore_signal(barrier, inc=1, device_id=(mate, f), device_id_type=MESH)

    @pl.when(jnp.logical_not(is_last))
    def _():
        pl.semaphore_signal(barrier, inc=1, device_id=(s + 1, f), device_id_type=MESH)

    @pl.when(jnp.logical_not(is_first))
    def _():
        pl.semaphore_signal(barrier, inc=1, device_id=(s - 1, f), device_id_type=MESH)

    load_fa.wait()
    for g in range(4):
        to = (g % 2) * 2 + g // 2
        for b in range(7):
            parts = [fa[t][:, 32 * g : 32 * g + 32] for t in range(4 * b, min(4 * b + 4, 27))]
            if len(parts) < 4:
                parts.append(jnp.zeros((64, 32), BF16))
            block = jnp.concatenate(parts, axis=1)
            for q in range(2):
                wa_send[to, q, :, 128 * b : 128 * b + 128] = block[32 * q : 32 * q + 32]

    at_end = jnp.logical_or(is_first, is_last)

    @pl.when(at_end)
    def _():
        pl.semaphore_wait(barrier, 5)

    @pl.when(jnp.logical_not(at_end))
    def _():
        pl.semaphore_wait(barrier, 6)

    def remote(src, dst, sems, target):
        return pltpu.make_async_remote_copy(
            src_ref=src, dst_ref=dst, send_sem=sems[0], recv_sem=sems[1],
            device_id=target, device_id_type=MESH,
        )

    def pair(sems, *index):
        return sems.at[(0,) + index], sems.at[(1,) + index]

    def slot_of(peer):
        return (peer % 2) * 2 + peer // 2

    def weight_copy(send, dst, sems, m):
        if m == 2 or send is wa_send or send is wb_send:
            return remote(send.at[slot_of(peers[m])], dst.at[slot], pair(sems, m), (s, peers[m]))
        return remote(
            send.at[slot_of(peers[m]), half], dst.at[slot, half], pair(sems, m), (s, peers[m])
        )

    def forward_copy(dst, sems, m):
        block = dst.at[slot_of(peers[m]), half]
        return remote(block, block, pair(sems, 3 + m), (mate, f))

    def forward(send, dst, sems):
        if send is wa_send or send is wb_send:
            return
        for m in range(2):
            weight_copy(send, dst, sems, m).wait_recv()
            forward_copy(dst, sems, m).start()

    def weights_here(send, dst, sems):
        weight_copy(send, dst, sems, 2).wait_recv()
        for m in range(2):
            if send is wa_send or send is wb_send:
                weight_copy(send, dst, sems, m).wait_recv()
                continue
            forward_copy(dst, sems, m).wait_recv()

    for m in range(3):
        weight_copy(wa_send, wa, wa_sems, m).start()
    wa[slot] = wa_send[slot]

    load_fb.wait()
    for g in range(4):
        to = (g % 2) * 2 + g // 2
        for b in range(14):
            parts = [fb[t][:, 64 * g : 64 * g + 64] for t in range(2 * b, min(2 * b + 2, 27))]
            if len(parts) < 2:
                parts.append(jnp.zeros((64, 64), BF16))
            block = jnp.concatenate(parts, axis=1)
            for q in range(2):
                wb_send[to, q, :, 128 * b : 128 * b + 128] = block[32 * q : 32 * q + 32]
    for m in range(3):
        weight_copy(wb_send, wb, wb_sems, m).start()
    wb[slot] = wb_send[slot]

    load.wait()
    load_s1.wait()

    def by_slice(q, carry):
        lanes = pl.ds(pl.multiple_of(q * 512, 512), 512)
        rows = jnp.swapaxes(xv[:, :, lanes], 0, 1)
        for k in range(4):
            x[32 * k : 32 * k + 32, lanes] = rows[k]
        return carry

    lax.fori_loop(0, 16, by_slice, 0)
    halo = remote(x.at[pl.ds(96, 32)], xh, pair(halo_sems), (s + 1, f))

    @pl.when(jnp.logical_not(is_last))
    def _():
        halo.start()


    def rows_of(ref, t):
        def row(r):
            return ref[:, pl.ds(pl.multiple_of(r * 128, 128), 128)]

        before = jnp.where(t > 0, row(jnp.maximum(4 * t - 1, 0)), jnp.zeros((), BF16))
        one = row(4 * t + 1)
        return (
            jnp.concatenate([before, one], 1),
            jnp.concatenate([row(4 * t), row(4 * t + 2)], 1),
            jnp.concatenate([one, row(4 * t + 3)], 1),
        )

    def taps_own(t, carry):
        cells = jnp.concatenate(rows_of(x, t), 0)
        picked = jnp.dot(cells, s1[...], preferred_element_type=F32).astype(BF16)
        lanes = pl.ds(pl.multiple_of(t * 128, 128), 128)
        for j in range(3):
            for l in range(3):
                for k in range(4):
                    piece = picked[j * 128 + k * 32 : j * 128 + k * 32 + 32, l * 128 : l * 128 + 128]
                    if k > 0:
                        at = ((k - 1) * 9 + 3 * j + l) * 32
                        v1[at : at + 32, lanes] = piece
                    if k < 2:
                        at = ((k + 1) * 9 + 3 * j + l) * 32
                        v0[at : at + 32, lanes] = piece
        return carry

    v0[864:896] = jnp.zeros((32, HALF), BF16)
    v1[864:896] = jnp.zeros((32, HALF), BF16)
    lax.fori_loop(0, 12, taps_own, 0, unroll=4)
    forward(wa_send, wa, wa_sems)
    lax.fori_loop(12, 16, taps_own, 0, unroll=4)

    def taps_halo(q, carry):
        cells = jnp.concatenate([c for t in range(4) for c in rows_of(xh, 4 * q + t)], 0)
        picked = jnp.dot(cells, s1[...], preferred_element_type=F32).astype(BF16)
        for t in range(4):
            lanes = pl.ds(pl.multiple_of((4 * q + t) * 128, 128), 128)
            for j in range(3):
                for l in range(3):
                    at = (3 * j + l) * 32
                    row = (3 * t + j) * 32
                    v0[at : at + 32, lanes] = picked[row : row + 32, l * 128 : l * 128 + 128]
        return carry

    def sib_copy(h, u):
        return remote(part.at[h, u, 1 - core], sib.at[h, u], pair(sib_sems, h, u), (s, sibling))

    def y_copy(h, u):
        return remote(y_send.at[h, u], y_recv.at[h, u], pair(y_sems, h, u), (s, partner))

    def across_one(h, u):
        sib_copy(h, u).wait_recv()
        y_send[h, u] = (part[h, u, core, 1 - chip] + sib[h, u, 1 - chip]).astype(BF16)
        y_copy(h, u).start()

    def across(h):
        across_one(h, 5)
        across_one(h, 6)
        across_one(h, 7)

    def first_conv(h, v):
        def body(u, carry):
            lanes = pl.ds(pl.multiple_of(u * 256, 256), 256)
            sums = jnp.dot(wa[...].reshape(256, 896), v[:, lanes], preferred_element_type=F32)
            part[h, u] = sums.reshape(2, 2, 64, 256)
            sib_copy(h, u).start()

            @pl.when(u >= 3)
            def _():
                across_one(h, u - 3)

            return carry

        lax.fori_loop(0, 8, body, 0)

    def hid_copy(u):
        return remote(hid.at[2, u], hid.at[0, u], pair(hid_sems, u), (s + 1, f))

    def finish(h, slot_h):
        bias = column(ba)

        def body(u, carry):
            y_copy(h, u).wait_recv()
            total = part[h, u, core, chip] + sib[h, u, chip] + y_recv[h, u].astype(F32) + bias
            hid[slot_h, u] = leaky(total)
            if slot_h == 2:

                @pl.when(jnp.logical_not(is_last))
                def _():
                    hid_copy(u).start()

            return carry

        lax.fori_loop(0, 8, body, 0)

    def second_taps(i):
        def block(q):
            return hid[i, q // 2, :, 128 * (q % 2) : 128 * (q % 2) + 128]

        zero = jnp.zeros((64, 128), BF16)
        now = jnp.concatenate(
            [jnp.concatenate([block(4 * u + r) for r in range(4)], 1) for u in range(4)], 0
        )
        before = jnp.concatenate(
            [
                jnp.concatenate([block(4 * u + r - 1) if 4 * u + r else zero for r in range(4)], 1)
                for u in range(4)
            ],
            0,
        )
        for j, (cells, half) in enumerate(((before, 1), (now, 0), (now, 1))):
            picked = jnp.dot(cells, s2[half], preferred_element_type=F32).astype(BF16)
            for u in range(4):
                for l in range(3):
                    at = (i * 9 + 3 * j + l) * 64
                    v2[at : at + 64, 128 * u : 128 * u + 128] = picked[
                        64 * u : 64 * u + 64, 128 * l : 128 * l + 128
                    ]

    weights_here(wa_send, wa, wa_sems)
    first_conv(1, v1)
    forward(wb_send, wb, wb_sems)

    @pl.when(is_first)
    def _():
        xh[...] = jnp.zeros(xh.shape, BF16)

    @pl.when(jnp.logical_not(is_first))
    def _():
        halo.wait_recv()

    load_ba.wait()
    across(1)
    lax.fori_loop(0, 4, taps_halo, 0)
    first_conv(0, v0)
    across(0)
    finish(1, 2)
    v2[1728:1792] = jnp.zeros((64, QUARTER), BF16)
    load_s2.wait()
    second_taps(2)
    finish(0, 1)
    second_taps(1)

    @pl.when(is_first)
    def _():
        hid[0] = jnp.zeros((8, 64, 256), BF16)

    @pl.when(jnp.logical_not(is_first))
    def _():
        for u in range(8):
            hid_copy(u).wait_recv()

    second_taps(0)
    weights_here(wb_send, wb, wb_sems)

    def sib2_copy(u):
        block = part2.at[u, 1 - core, chip]
        return remote(block, sib2.at[u], pair(sib2_sems, u), (s, sibling))

    def z_copy(u, m):
        return remote(z_send.at[u, m], z_recv.at[u, m], pair(z_sems, u, m), (s, peers[m]))

    for u in range(2):
        lanes = slice(256 * u, 256 * u + 256)
        sums = jnp.dot(wb[...].reshape(256, 1792), v2[:, lanes], preferred_element_type=F32)
        part2[u] = sums.reshape(2, 2, 64, 256)
        for m in range(2):
            to_core = 1 - core if m == 0 else core
            z_send[u, m] = part2[u, to_core, 1 - chip].astype(BF16)
            z_copy(u, m).start()
        sib2_copy(u).start()
    load_bb.wait()
    bias = column(bb)
    for u in range(2):
        sib2_copy(u).wait_recv()
        for m in range(2):
            z_copy(u, m).wait_recv()
        far = z_recv[u, 0].astype(F32) + z_recv[u, 1].astype(F32)
        total = part2[u, core, chip] + sib2[u] + far + bias
        out[:, 256 * u : 256 * u + 256] = leaky(total)

    for m in range(3):
        weight_copy(wa_send, wa, wa_sems, m).wait_send()
        weight_copy(wb_send, wb, wb_sems, m).wait_send()
    for m in range(2):
        pass
        pass

    @pl.when(jnp.logical_not(is_last))
    def _():
        halo.wait_send()
        for u in range(8):
            hid_copy(u).wait_send()

    for h in range(2):

        def drain(u, carry, h=h):
            sib_copy(h, u).wait_send()
            y_copy(h, u).wait_send()
            return carry

        lax.fori_loop(0, 8, drain, 0)
    for u in range(2):
        sib2_copy(u).wait_send()
        for m in range(2):
            z_copy(u, m).wait_send()


def scattered(n_spatial, volume_in, filters_a, bias_a, filters_b, bias_b):
    vmem = pl.BlockSpec(memory_space=pltpu.VMEM)
    hbm = pl.BlockSpec(memory_space=pltpu.HBM)
    dma = pltpu.SemaphoreType.DMA

    def body(*refs):
        kernel(n_spatial, *refs)

    out = pl.pallas_call(
        body,
        out_shape=jax.ShapeDtypeStruct((64, QUARTER), BF16),
        in_specs=[hbm] * 7,
        out_specs=vmem,
        scratch_shapes=[
            pltpu.VMEM((27, 64, 128), BF16),
            pltpu.VMEM((1, 64), BF16),
            pltpu.VMEM((1, 64), BF16),
            pltpu.VMEM((27, 64, 256), BF16),
            pltpu.VMEM((256, 384), BF16),
            pltpu.VMEM((2, 512, 384), BF16),
            pltpu.VMEM((32, 4, ROWS * COLS), BF16),
            pltpu.VMEM((128, ROWS * COLS), BF16),
            pltpu.VMEM((32, ROWS * COLS), BF16),
            pltpu.VMEM((4, 2, 32, 896), BF16),
            pltpu.VMEM((4, 2, 32, 896), BF16),
            pltpu.VMEM((4, 2, 32, 1792), BF16),
            pltpu.VMEM((4, 2, 32, 1792), BF16),
            pltpu.VMEM((896, HALF), BF16),
            pltpu.VMEM((896, HALF), BF16),
            pltpu.VMEM((2, 8, 2, 2, 64, 256), F32),
            pltpu.VMEM((2, 8, 2, 64, 256), F32),
            pltpu.VMEM((2, 8, 64, 256), BF16),
            pltpu.VMEM((2, 8, 64, 256), BF16),
            pltpu.VMEM((3, 8, 64, 256), BF16),
            pltpu.VMEM((1792, QUARTER), BF16),
            pltpu.VMEM((2, 2, 2, 64, 256), F32),
            pltpu.VMEM((2, 64, 256), F32),
            pltpu.VMEM((2, 2, 64, 256), BF16),
            pltpu.VMEM((2, 2, 64, 256), BF16),
            dma((6,)), dma, dma((2,)), dma((2, 5)), dma((2, 5)), dma((2, 2, 8)), dma((2, 2, 8)), dma((2, 8)),
            dma((2, 2)), dma((2, 2, 2)),
        ],
        compiler_params=pltpu.CompilerParams(
            collective_id=0, has_side_effects=True, vmem_limit_bytes=56 * 1024 * 1024
        ),
        name="scattered_convs",
    )(
        volume_in,
        filters_a,
        filters_b,
        bias_a.reshape(1, 64),
        bias_b.reshape(1, 64),
        jnp.asarray(pick_first(), BF16),
        jnp.asarray(pick_second(), BF16),
    )
    return out.reshape(64, 1, QUARTER)


def per_device(volume_in, filters_a, bias_a, filters_b, bias_b):
    n_spatial = lax.axis_size("spatial")
    own = volume_in.shape == (32, 4, ROWS * COLS) and filters_b.shape == (27, 64, 256)
    if own and n_spatial % 4 == 0:
        return scattered(n_spatial, volume_in, filters_a, bias_a, filters_b, bias_b)
    return gathered(volume_in, filters_a, bias_a, filters_b, bias_b)


def solution(mesh):
    in_specs = (
        P("filter", "spatial", None),
        P(None, "filter", None),
        P("filter"),
        P(None, "filter", None),
        P("filter"),
    )
    return jax.shard_map(
        per_device,
        mesh=mesh,
        in_specs=in_specs,
        out_specs=P("filter", "spatial", None),
        check_vma=False,
    )
```

```python
import jax
import jax.numpy as jnp
import numpy as np
from jax import lax
from jax.experimental import pallas as pl
from jax.experimental.pallas import tpu as pltpu
from jax.sharding import PartitionSpec as P

MESH = pl.DeviceIdType.MESH
ROWS = 64
COLS = 128
F32 = jnp.float32
BF16 = jnp.bfloat16


def shifted(block, axis, distance):
    devices = range(lax.axis_size(axis))
    route = [(i - distance, i) for i in devices if i - distance in devices]
    return lax.ppermute(block, axis, route)


def local_conv(block, weight, pad_rows, row_count, col_count):
    channels = block.shape[0]
    slices = block.shape[1]
    volume = block.reshape(1, channels, slices, row_count, col_count)
    kernel = weight.reshape(3, 3, 3, weight.shape[1], weight.shape[2])
    return lax.conv_general_dilated(
        volume,
        kernel,
        (2, 2, 2),
        ((0, 0), (pad_rows, pad_rows), (1, 1)),
        dimension_numbers=("NCDHW", "DHWOI", "NCDHW"),
        preferred_element_type=F32,
    )[0]


def activate(summed, bias_vec):
    summed = summed + bias_vec.astype(F32)[:, None, None, None]
    return jnp.where(summed > 0, summed, 0.2 * summed).astype(BF16)


def gathered(volume_in, filters_a, bias_a, filters_b, bias_b):
    slices = volume_in.shape[1]
    outputs = filters_a.shape[1]
    extended = jnp.concatenate([shifted(volume_in[:, -1:], "spatial", 1), volume_in], 1)
    full = lax.all_gather(extended, "filter", axis=0, tiled=True)
    hidden = activate(local_conv(full, filters_a, 1, ROWS, COLS), bias_a)
    hidden = hidden.reshape(outputs, slices // 2, ROWS // 2 * (COLS // 2))
    extended = jnp.concatenate([shifted(hidden[:, -1:], "spatial", 1), hidden], 1)
    full = lax.all_gather(extended, "filter", axis=0, tiled=True)
    out = activate(local_conv(full, filters_b, 1, ROWS // 2, COLS // 2), bias_b)
    return out.reshape(filters_b.shape[1], slices // 4, ROWS // 4 * (COLS // 4))


HALF = 2048
QUARTER = 512


def pick_first():
    s = np.zeros((256, 3, 128), np.float32)
    for l in range(3):
        for row in range(2):
            for w in range(64):
                source = 2 * w + l - 1
                if source >= 0:
                    s[row * 128 + source, l, row * 64 + w] = 1
    return s.reshape(256, 384)


def pick_second():
    s = np.zeros((2, 512, 3, 128), np.float32)
    for half in range(2):
        for l in range(3):
            for row in range(4):
                for w in range(32):
                    source = 2 * w + l - 1
                    if source >= 0:
                        s[half, row * 128 + half * 64 + source, l, row * 32 + w] = 1
    return s.reshape(2, 512, 384)


def column(row_ref):
    row = lax.broadcasted_iota(jnp.int32, (64, 64), 0)
    col = lax.broadcasted_iota(jnp.int32, (64, 64), 1)
    spread = jnp.broadcast_to(row_ref[...].astype(F32), (64, 64))
    diagonal = jnp.where(row == col, spread, 0.0).astype(BF16)
    return jnp.dot(diagonal, jnp.ones((64, 256), BF16), preferred_element_type=F32)


def leaky(u):
    return jnp.where(u > 0, u, 0.2 * u).astype(BF16)


WA_MODE = "full"
WB_MODE = "quad"
TAPS_B = tuple(range(9)) + tuple(range(18, 27)) + tuple(range(9, 18))


def kernel(
    n_spatial, xin, fa_in, fb_in, ba_in, bb_in, s1_in, s2_in, out,
    fa, ba, bb, fb, s1, s2, xv, x, xh, wa_send, wa, wb_send, wb, v0, v1, part, sib, y_send, y_recv, hid, v2,
    part2, sib2, z_send, z_recv,
    in_sems, x_sems, halo_sems, wa_sems, wb_sems, sib_sems, y_sems, hid_sems, sib2_sems, z_sems,
):
    scope = jax.named_scope
    s = lax.axis_index("spatial")
    f = lax.axis_index("filter")
    core, chip = f % 2, f // 2
    sibling = chip * 2 + (1 - core)
    partner = (1 - chip) * 2 + core
    diagonal = (1 - chip) * 2 + (1 - core)
    slot = core * 2 + chip
    peers = (diagonal, partner, sibling)
    is_first, is_last = s == 0, s == n_spatial - 1
    even, upper = s % 2, (s // 2) % 2
    mate_x = s + 1 - 2 * even
    mate_z = s + 2 - 4 * upper
    quarter = 2 * upper + even
    quarter_x = 2 * upper + 1 - even

    load_fa = pltpu.make_async_copy(fa_in, fa, in_sems.at[3])
    load_fa.start()

    def x_load(c):
        lanes = pl.ds(pl.multiple_of(c * 2048, 2048), 2048)
        return pltpu.make_async_copy(xin.at[:, :, lanes], xv.at[:, :, lanes], x_sems.at[c])

    for c in range(4):
        x_load(c).start()
    load_s1 = pltpu.make_async_copy(s1_in, s1, in_sems.at[1])
    load_fb = pltpu.make_async_copy(fb_in, fb, in_sems.at[0])
    load_ba = pltpu.make_async_copy(ba_in, ba, in_sems.at[4])
    load_bb = pltpu.make_async_copy(bb_in, bb, in_sems.at[5])
    load_s2 = pltpu.make_async_copy(s2_in, s2, in_sems.at[2])
    load_s1.start()
    load_fb.start()
    load_ba.start()
    load_bb.start()
    load_s2.start()
    barrier = pltpu.get_barrier_semaphore()
    for peer in peers:
        pl.semaphore_signal(barrier, inc=1, device_id=(s, peer), device_id_type=MESH)
    pl.semaphore_signal(barrier, inc=1, device_id=(mate_z, f), device_id_type=MESH)

    @pl.when(jnp.logical_not(is_last))
    def _():
        pl.semaphore_signal(barrier, inc=1, device_id=(s + 1, f), device_id_type=MESH)

    @pl.when(jnp.logical_not(is_first))
    def _():
        pl.semaphore_signal(barrier, inc=1, device_id=(s - 1, f), device_id_type=MESH)

    with scope("load_fa"):
        load_fa.wait()
    with scope("pack_a"):
        for g in range(4):
            to = (g % 2) * 2 + g // 2
            for b in range(7):
                parts = [fa[t][:, 32 * g : 32 * g + 32] for t in range(4 * b, min(4 * b + 4, 27))]
                if len(parts) < 4:
                    parts.append(jnp.zeros((64, 32), BF16))
                block = jnp.concatenate(parts, axis=1)
                for q in range(2):
                    wa_send[to, q, :, 128 * b : 128 * b + 128] = block[32 * q : 32 * q + 32]

    at_end = jnp.logical_or(is_first, is_last)
    with scope("barrier"):

        @pl.when(at_end)
        def _():
            pl.semaphore_wait(barrier, 5)

        @pl.when(jnp.logical_not(at_end))
        def _():
            pl.semaphore_wait(barrier, 6)

    def remote(src, dst, sems, target):
        return pltpu.make_async_remote_copy(
            src_ref=src, dst_ref=dst, send_sem=sems[0], recv_sem=sems[1],
            device_id=target, device_id_type=MESH,
        )

    def pair(sems, *index):
        return sems.at[(0,) + index], sems.at[(1,) + index]

    def slot_of(peer):
        return (peer % 2) * 2 + peer // 2

    def whole(send, dst, sems, m):
        return remote(send.at[slot_of(peers[m])], dst.at[slot], pair(sems, m), (s, peers[m]))

    def piece(send, dst, sems, m, q):
        return remote(send.at[slot_of(peers[m]), q], dst.at[slot, q], pair(sems, m), (s, peers[m]))

    def passed(dst, sems, m, q, k, mate):
        block = dst.at[slot_of(peers[m]), q]
        return remote(block, block, pair(sems, k + m), (mate, f))

    if WA_MODE == "full":
        a_first = [whole(wa_send, wa, wa_sems, m) for m in range(2)]
        a_pass = []
    else:
        a_half = even if WA_MODE == "x" else upper
        a_mate = mate_x if WA_MODE == "x" else mate_z
        a_first = [piece(wa_send, wa, wa_sems, m, a_half) for m in range(2)]
        a_pass = [passed(wa, wa_sems, m, a_half, 3, a_mate) for m in range(2)]
    a_sib = whole(wa_send, wa, wa_sems, 2)
    b_first = [piece(wb_send, wb, wb_sems, m, quarter) for m in range(2)]
    b_x = [passed(wb, wb_sems, m, quarter, 3, mate_x) for m in range(2)]
    b_z = [passed(wb, wb_sems, m, quarter, 5, mate_z) for m in range(2)]
    b_xz = [passed(wb, wb_sems, m, quarter_x, 7, mate_z) for m in range(2)]
    b_sib = whole(wb_send, wb, wb_sems, 2)

    for copy in a_first:
        copy.start()
    a_sib.start()
    wa[slot] = wa_send[slot]

    def halo_copy(c):
        lanes = pl.ds(pl.multiple_of(c * 2048, 2048), 2048)
        return remote(x.at[pl.ds(96, 32), lanes], xh.at[:, lanes], pair(halo_sems, c), (s + 1, f))

    def by_slice(q):
        lanes = pl.ds(pl.multiple_of(q * 512, 512), 512)
        rows = jnp.swapaxes(xv[:, :, lanes], 0, 1)
        for k in range(4):
            x[32 * k : 32 * k + 32, lanes] = rows[k]

    with scope("slices"):

        def body(c, carry):
            x_load(c).wait()
            for q in range(4):
                by_slice(4 * c + q)

            @pl.when(jnp.logical_not(is_last))
            def _():
                halo_copy(c).start()

            return carry

        lax.fori_loop(0, 4, body, 0)

    with scope("pack_b"):
        load_fb.wait()
        for g in range(4):
            to = (g % 2) * 2 + g // 2
            for b in range(14):
                parts = [fb[t][:, 64 * g : 64 * g + 64] for t in TAPS_B[2 * b : 2 * b + 2]]
                if len(parts) < 2:
                    parts.append(jnp.zeros((64, 64), BF16))
                block = jnp.concatenate(parts, axis=1)
                for q in range(4):
                    wb_send[to, q, :, 128 * b : 128 * b + 128] = block[16 * q : 16 * q + 16]
        wb[slot] = wb_send[slot]

    def rows_of(ref, t):
        def row(r):
            return ref[:, pl.ds(pl.multiple_of(r * 128, 128), 128)]

        before = jnp.where(t > 0, row(jnp.maximum(4 * t - 1, 0)), jnp.zeros((), BF16))
        one = row(4 * t + 1)
        return (
            jnp.concatenate([before, one], 1),
            jnp.concatenate([row(4 * t), row(4 * t + 2)], 1),
            jnp.concatenate([one, row(4 * t + 3)], 1),
        )

    def taps_own(t, carry):
        cells = jnp.concatenate(rows_of(x, t), 0)
        picked = jnp.dot(cells, s1[...], preferred_element_type=F32).astype(BF16)
        lanes = pl.ds(pl.multiple_of(t * 128, 128), 128)
        for j in range(3):
            for l in range(3):
                for k in range(4):
                    piece = picked[j * 128 + k * 32 : j * 128 + k * 32 + 32, l * 128 : l * 128 + 128]
                    if k > 0:
                        at = ((k - 1) * 9 + 3 * j + l) * 32
                        v1[at : at + 32, lanes] = piece
                    if k < 2:
                        at = ((k + 1) * 9 + 3 * j + l) * 32
                        v0[at : at + 32, lanes] = piece
        return carry

    v0[864:896] = jnp.zeros((32, HALF), BF16)
    v1[864:896] = jnp.zeros((32, HALF), BF16)
    load_s1.wait()
    with scope("taps_a"):
        lax.fori_loop(0, 8, taps_own, 0, unroll=4)
    for m in range(len(a_pass)):
        with scope("pass_wa"):
            a_first[m].wait_recv()
            a_pass[m].start()
    with scope("taps_b"):
        lax.fori_loop(8, 16, taps_own, 0, unroll=4)

    def taps_halo(q):
        cells = jnp.concatenate([c for t in range(4) for c in rows_of(xh, 4 * q + t)], 0)
        picked = jnp.dot(cells, s1[...], preferred_element_type=F32).astype(BF16)
        for t in range(4):
            lanes = pl.ds(pl.multiple_of((4 * q + t) * 128, 128), 128)
            for j in range(3):
                for l in range(3):
                    at = (3 * j + l) * 32
                    row = (3 * t + j) * 32
                    v0[at : at + 32, lanes] = picked[row : row + 32, l * 128 : l * 128 + 128]

    def sib_copy(h, u):
        return remote(part.at[h, u, 1 - core], sib.at[h, u], pair(sib_sems, h, u), (s, sibling))

    def y_copy(h, u):
        return remote(y_send.at[h, u], y_recv.at[h, u], pair(y_sems, h, u), (s, partner))

    def across(h, c):
        for k in range(2):
            u = 2 * c + k
            sib_copy(h, u).wait_recv()
            y_send[h, u] = (part[h, u, core, 1 - chip] + sib[h, u, 1 - chip]).astype(BF16)
            y_copy(h, u).start()

    def first_conv(h, v, c):
        lanes = pl.ds(pl.multiple_of(c * 512, 512), 512)
        sums = jnp.dot(wa[...].reshape(256, 896), v[:, lanes], preferred_element_type=F32)
        for k in range(2):
            u = 2 * c + k
            part[h, u] = sums[:, 256 * k : 256 * k + 256].reshape(2, 2, 64, 256)
            sib_copy(h, u).start()

    def hid_copy(u):
        return remote(hid.at[2, u], hid.at[0, u], pair(hid_sems, u), (s + 1, f))

    load_ba.wait()
    bias_a = column(ba)

    def finish(h, slot_h, u):
        y_copy(h, u).wait_recv()
        total = part[h, u, core, chip] + sib[h, u, chip] + y_recv[h, u].astype(F32) + bias_a
        hid[slot_h, u] = leaky(total)
        if slot_h == 2:

            @pl.when(jnp.logical_not(is_last))
            def _():
                hid_copy(u).start()

    def second_taps(i, at_i, quarters):
        def block(q):
            return hid[i, q // 2, :, 128 * (q % 2) : 128 * (q % 2) + 128]

        zero = jnp.zeros((64, 128), BF16)
        now = jnp.concatenate(
            [jnp.concatenate([block(4 * u + r) for r in range(4)], 1) for u in quarters], 0
        )
        before = jnp.concatenate(
            [
                jnp.concatenate([block(4 * u + r - 1) if 4 * u + r else zero for r in range(4)], 1)
                for u in quarters
            ],
            0,
        )
        for j, (cells, half) in enumerate(((before, 1), (now, 0), (now, 1))):
            picked = jnp.dot(cells, s2[half], preferred_element_type=F32).astype(BF16)
            for n, u in enumerate(quarters):
                for l in range(3):
                    at = (at_i * 9 + 3 * j + l) * 64
                    v2[at : at + 64, 128 * u : 128 * u + 128] = picked[
                        64 * n : 64 * n + 64, 128 * l : 128 * l + 128
                    ]

    with scope("wait_wa"):
        a_sib.wait_recv()
        if a_pass:
            for copy in a_pass:
                copy.wait_recv()
        else:
            for copy in a_first:
                copy.wait_recv()
    for copy in b_first:
        copy.start()
    b_sib.start()

    with scope("conv_d1"):
        first_conv(1, v1, 0)

        def body(c, carry):
            first_conv(1, v1, c)
            across(1, c - 1)
            return carry

        lax.fori_loop(1, 4, body, 0)
        across(1, 3)

    with scope("pass_wb"):
        for m in range(2):
            b_first[m].wait_recv()
            b_x[m].start()
            b_z[m].start()

    @pl.when(is_first)
    def _():
        xh[...] = jnp.zeros(xh.shape, BF16)

    def halo_here(c):
        @pl.when(jnp.logical_not(is_first))
        def _():
            halo_copy(c).wait_recv()

    with scope("conv_d0_0"):
        halo_here(0)
        taps_halo(0)
        first_conv(0, v0, 0)

    def rest(c, carry):
        with scope("halo_wait"):
            halo_here(c)
        with scope("taps_halo"):
            taps_halo(c)
        with scope("conv_d0"):
            first_conv(0, v0, c)
            across(0, c - 1)
        return carry

    def finish_some(c):
        with scope("finish_d1"):
            for k in range(2):
                finish(1, 2, 2 * c + k)

    lax.fori_loop(1, 3, rest, 0)
    finish_some(0)
    finish_some(1)
    rest(3, 0)
    with scope("across_3"):
        across(0, 3)
    with scope("pass_wb_xz"):
        for m in range(2):
            b_x[m].wait_recv()
            b_xz[m].start()
    finish_some(2)
    finish_some(3)
    load_s2.wait()
    with scope("taps2_d1"):
        v2[1728:1792] = jnp.zeros((64, QUARTER), BF16)
        second_taps(2, 1, range(4))

    @pl.when(is_first)
    def _():
        hid[0] = jnp.zeros((8, 64, 256), BF16)

    with scope("hid_wait"):

        @pl.when(jnp.logical_not(is_first))
        def _():
            for u in range(8):
                hid_copy(u).wait_recv()

    with scope("taps2_halo"):
        second_taps(0, 0, range(4))
    with scope("wait_wb"):
        b_sib.wait_recv()
        for m in range(2):
            b_z[m].wait_recv()
            b_xz[m].wait_recv()
    with scope("conv2_sides"):
        sums = jnp.dot(
            wb[:, :, :, :1152].reshape(256, 1152), v2[:1152], preferred_element_type=F32
        )
        for u in range(2):
            part2[u] = sums[:, 256 * u : 256 * u + 256].reshape(2, 2, 64, 256)

    def sib2_copy(u):
        block = part2.at[u, 1 - core, chip]
        return remote(block, sib2.at[u], pair(sib2_sems, u), (s, sibling))

    def z_copy(u, m):
        return remote(z_send.at[u, m], z_recv.at[u, m], pair(z_sems, u, m), (s, peers[m]))

    for u in range(2):
        with scope("finish_d0"):
            for k in range(4):
                finish(0, 1, 4 * u + k)
        with scope("conv2_mid"):
            second_taps(1, 2, range(2 * u, 2 * u + 2))
            lanes = slice(256 * u, 256 * u + 256)
            sums = jnp.dot(
                wb[:, :, :, 1152:].reshape(256, 640), v2[1152:, lanes], preferred_element_type=F32
            )
            part2[u] = part2[u] + sums.reshape(2, 2, 64, 256)
            for m in range(2):
                to_core = 1 - core if m == 0 else core
                z_send[u, m] = part2[u, to_core, 1 - chip].astype(BF16)
                z_copy(u, m).start()
            sib2_copy(u).start()
    load_bb.wait()
    bias = column(bb)
    for u in range(2):
        with scope("z_wait"):
            sib2_copy(u).wait_recv()
            for m in range(2):
                z_copy(u, m).wait_recv()
        far = z_recv[u, 0].astype(F32) + z_recv[u, 1].astype(F32)
        total = part2[u, core, chip] + sib2[u] + far + bias
        out[:, 256 * u : 256 * u + 256] = leaky(total)

    with scope("drain"):
        for copy in a_first + a_pass + [a_sib] + b_first + b_x + b_z + b_xz + [b_sib]:
            copy.wait_send()

        @pl.when(jnp.logical_not(is_last))
        def _():
            for c in range(4):
                halo_copy(c).wait_send()
            for u in range(8):
                hid_copy(u).wait_send()

        for h in range(2):

            def drain(u, carry, h=h):
                sib_copy(h, u).wait_send()
                y_copy(h, u).wait_send()
                return carry

            lax.fori_loop(0, 8, drain, 0)
        for u in range(2):
            sib2_copy(u).wait_send()
            for m in range(2):
                z_copy(u, m).wait_send()


def scattered(n_spatial, volume_in, filters_a, bias_a, filters_b, bias_b):
    vmem = pl.BlockSpec(memory_space=pltpu.VMEM)
    hbm = pl.BlockSpec(memory_space=pltpu.HBM)
    dma = pltpu.SemaphoreType.DMA

    def body(*refs):
        kernel(n_spatial, *refs)

    out = pl.pallas_call(
        body,
        out_shape=jax.ShapeDtypeStruct((64, QUARTER), BF16),
        in_specs=[hbm] * 7,
        out_specs=vmem,
        scratch_shapes=[
            pltpu.VMEM((27, 64, 128), BF16),
            pltpu.VMEM((1, 64), BF16),
            pltpu.VMEM((1, 64), BF16),
            pltpu.VMEM((27, 64, 256), BF16),
            pltpu.VMEM((256, 384), BF16),
            pltpu.VMEM((2, 512, 384), BF16),
            pltpu.VMEM((32, 4, ROWS * COLS), BF16),
            pltpu.VMEM((128, ROWS * COLS), BF16),
            pltpu.VMEM((32, ROWS * COLS), BF16),
            pltpu.VMEM((4, 2, 32, 896), BF16),
            pltpu.VMEM((4, 2, 32, 896), BF16),
            pltpu.VMEM((4, 4, 16, 1792), BF16),
            pltpu.VMEM((4, 4, 16, 1792), BF16),
            pltpu.VMEM((896, HALF), BF16),
            pltpu.VMEM((896, HALF), BF16),
            pltpu.VMEM((2, 8, 2, 2, 64, 256), F32),
            pltpu.VMEM((2, 8, 2, 64, 256), F32),
            pltpu.VMEM((2, 8, 64, 256), BF16),
            pltpu.VMEM((2, 8, 64, 256), BF16),
            pltpu.VMEM((3, 8, 64, 256), BF16),
            pltpu.VMEM((1792, QUARTER), BF16),
            pltpu.VMEM((2, 2, 2, 64, 256), F32),
            pltpu.VMEM((2, 64, 256), F32),
            pltpu.VMEM((2, 2, 64, 256), BF16),
            pltpu.VMEM((2, 2, 64, 256), BF16),
            dma((6,)), dma((4,)), dma((2, 4)), dma((2, 5)), dma((2, 9)), dma((2, 2, 8)), dma((2, 2, 8)), dma((2, 8)),
            dma((2, 2)), dma((2, 2, 2)),
        ],
        compiler_params=pltpu.CompilerParams(
            collective_id=0, has_side_effects=True, vmem_limit_bytes=52 * 1024 * 1024
        ),
        name="scattered_convs",
    )(
        *(
            pltpu.with_memory_space_constraint(a, pltpu.HBM)
            for a in (
                volume_in,
                filters_a,
                filters_b,
                bias_a.reshape(1, 64),
                bias_b.reshape(1, 64),
                jnp.asarray(pick_first(), BF16),
                jnp.asarray(pick_second(), BF16),
            )
        )
    )
    return out.reshape(64, 1, QUARTER)


def per_device(volume_in, filters_a, bias_a, filters_b, bias_b):
    n_spatial = lax.axis_size("spatial")
    own = volume_in.shape == (32, 4, ROWS * COLS) and filters_b.shape == (27, 64, 256)
    if own and n_spatial % 4 == 0:
        return scattered(n_spatial, volume_in, filters_a, bias_a, filters_b, bias_b)
    return gathered(volume_in, filters_a, bias_a, filters_b, bias_b)


def solution(mesh):
    in_specs = (
        P("filter", "spatial", None),
        P(None, "filter", None),
        P("filter"),
        P(None, "filter", None),
        P("filter"),
    )
    return jax.shard_map(
        per_device,
        mesh=mesh,
        in_specs=in_specs,
        out_specs=P("filter", "spatial", None),
        check_vma=False,
    )
```

```python
import jax
import jax.numpy as jnp
import numpy as np
from jax import lax
from jax.experimental import pallas as pl
from jax.experimental.pallas import tpu as pltpu
from jax.sharding import PartitionSpec as P

MESH = pl.DeviceIdType.MESH
ROWS = 64
COLS = 128
F32 = jnp.float32
BF16 = jnp.bfloat16


def shifted(block, axis, distance):
    devices = range(lax.axis_size(axis))
    route = [(i - distance, i) for i in devices if i - distance in devices]
    return lax.ppermute(block, axis, route)


def local_conv(block, weight, pad_rows, row_count, col_count):
    channels = block.shape[0]
    slices = block.shape[1]
    volume = block.reshape(1, channels, slices, row_count, col_count)
    kernel = weight.reshape(3, 3, 3, weight.shape[1], weight.shape[2])
    return lax.conv_general_dilated(
        volume,
        kernel,
        (2, 2, 2),
        ((0, 0), (pad_rows, pad_rows), (1, 1)),
        dimension_numbers=("NCDHW", "DHWOI", "NCDHW"),
        preferred_element_type=F32,
    )[0]


def activate(summed, bias_vec):
    summed = summed + bias_vec.astype(F32)[:, None, None, None]
    return jnp.where(summed > 0, summed, 0.2 * summed).astype(BF16)


def gathered(volume_in, filters_a, bias_a, filters_b, bias_b):
    slices = volume_in.shape[1]
    outputs = filters_a.shape[1]
    extended = jnp.concatenate([shifted(volume_in[:, -1:], "spatial", 1), volume_in], 1)
    full = lax.all_gather(extended, "filter", axis=0, tiled=True)
    hidden = activate(local_conv(full, filters_a, 1, ROWS, COLS), bias_a)
    hidden = hidden.reshape(outputs, slices // 2, ROWS // 2 * (COLS // 2))
    extended = jnp.concatenate([shifted(hidden[:, -1:], "spatial", 1), hidden], 1)
    full = lax.all_gather(extended, "filter", axis=0, tiled=True)
    out = activate(local_conv(full, filters_b, 1, ROWS // 2, COLS // 2), bias_b)
    return out.reshape(filters_b.shape[1], slices // 4, ROWS // 4 * (COLS // 4))


HALF = 2048
QUARTER = 512


def pick_first():
    s = np.zeros((256, 3, 128), np.float32)
    for l in range(3):
        for row in range(2):
            for w in range(64):
                source = 2 * w + l - 1
                if source >= 0:
                    s[row * 128 + source, l, row * 64 + w] = 1
    return s.reshape(256, 384)


def pick_second():
    s = np.zeros((2, 512, 3, 128), np.float32)
    for half in range(2):
        for l in range(3):
            for row in range(4):
                for w in range(32):
                    source = 2 * w + l - 1
                    if source >= 0:
                        s[half, row * 128 + half * 64 + source, l, row * 32 + w] = 1
    return s.reshape(2, 512, 384)


def column(row_of):
    row = lax.broadcasted_iota(jnp.int32, (64, 64), 0)
    col = lax.broadcasted_iota(jnp.int32, (64, 64), 1)
    spread = jnp.broadcast_to(row_of.astype(F32), (64, 64))
    diagonal = jnp.where(row == col, spread, 0.0).astype(BF16)
    return jnp.dot(diagonal, jnp.ones((64, 512), BF16), preferred_element_type=F32)


def leaky(u):
    return jnp.where(u > 0, u, 0.2 * u).astype(BF16)


TAPS_B = tuple(range(9)) + tuple(range(18, 27)) + tuple(range(9, 18))


def kernel(
    n_spatial, xin, fa_in, fb_in, ba_in, bb_in, s1_in, s2_in, out,
    fa, biases, fb, s1, s2, xv, x, xh, wa_send, wa, wb_send, wb, v0, v1, part, sib, y_send, y_recv, hid, v2,
    part2, sib2, z_send, z_recv,
    in_sems, x_sems, send_sems, halo_sems, wa_sem, wb_sems, sib_sems, y_sems, hid_sem, sib2_sems, z_sems,
):
    scope = jax.named_scope
    s = lax.axis_index("spatial")
    f = lax.axis_index("filter")
    core, chip = f % 2, f // 2
    sibling = chip * 2 + (1 - core)
    partner = (1 - chip) * 2 + core
    diagonal = (1 - chip) * 2 + (1 - core)
    slot = core * 2 + chip
    peers = (diagonal, partner, sibling)
    is_first, is_last = s == 0, s == n_spatial - 1
    is_even = s % 2 == 0
    level = (s // 2) % 4
    half = level % 2
    is_odd = s % 2 == 1
    passes_down = level > 0
    even_up = jnp.logical_and(is_even, level == 2)
    odd_up = jnp.logical_and(is_odd, level == 2)
    from_corner = jnp.logical_and(is_odd, level == 3)

    halo_sent, wa_sent, wb_sent, sib_sent, y_sent, hid_sent, sib2_sent, z_sent = (
        send_sems.at[k] for k in range(8)
    )
    load_fa = pltpu.make_async_copy(fa_in, fa, in_sems.at[3])
    load_fa.start()

    def x_load(c):
        lanes = pl.ds(pl.multiple_of(c * 2048, 2048), 2048)
        return pltpu.make_async_copy(xin.at[:, :, lanes], xv.at[:, :, lanes], x_sems.at[c])

    for c in range(4):
        x_load(c).start()
    load_s1 = pltpu.make_async_copy(s1_in, s1, in_sems.at[1])
    load_fb = pltpu.make_async_copy(fb_in, fb, in_sems.at[0])
    load_ba = pltpu.make_async_copy(ba_in, biases.at[0], in_sems.at[4])
    load_bb = pltpu.make_async_copy(bb_in, biases.at[1], in_sems.at[4])
    load_s2 = pltpu.make_async_copy(s2_in, s2, in_sems.at[2])
    load_s1.start()
    load_fb.start()
    load_ba.start()
    load_bb.start()
    load_s2.start()
    barrier = pltpu.get_barrier_semaphore()
    for peer in peers:
        pl.semaphore_signal(barrier, inc=1, device_id=(s, peer), device_id_type=MESH)
    for step in (1, 2):

        @pl.when(s < n_spatial - step)
        def _():
            pl.semaphore_signal(barrier, inc=1, device_id=(s + step, f), device_id_type=MESH)

        @pl.when(s >= step)
        def _():
            pl.semaphore_signal(barrier, inc=1, device_id=(s - step, f), device_id_type=MESH)

    @pl.when(from_corner)
    def _():
        pl.semaphore_signal(barrier, inc=1, device_id=(s - 3, f), device_id_type=MESH)

    with scope("load_fa"):
        load_fa.wait()
    with scope("pack_a"):
        for g in range(4):
            to = (g % 2) * 2 + g // 2
            for b in range(7):
                parts = [fa[t][:, 32 * g : 32 * g + 32] for t in range(4 * b, min(4 * b + 4, 27))]
                if len(parts) < 4:
                    parts.append(jnp.zeros((64, 32), BF16))
                block = jnp.concatenate(parts, axis=1)
                for q in range(2):
                    wa_send[to, q, :, 128 * b : 128 * b + 128] = block[32 * q : 32 * q + 32]

    with scope("barrier"):
        neighbours = jnp.minimum(s, 2) + jnp.minimum(n_spatial - 1 - s, 2)
        pl.semaphore_wait(barrier, 3 + neighbours + jnp.where(even_up, 1, 0))

    def remote(src, dst, sent, here, target):
        return pltpu.make_async_remote_copy(
            src_ref=src, dst_ref=dst, send_sem=sent, recv_sem=here,
            device_id=target, device_id_type=MESH,
        )

    def slot_of(peer):
        return (peer % 2) * 2 + peer // 2

    near = (s, sibling)

    def to_sibling(send, dst, sent, here):
        return remote(send.at[slot_of(sibling)], dst.at[slot], sent, here, near)

    def own_half(m):
        return remote(
            wb_send.at[slot_of(peers[m]), half], wb.at[slot, half], wb_sent, wb_sems.at[m],
            (s, peers[m]),
        )

    def pass_on(m):
        block = wb.at[slot_of(peers[m]), half]

        def to(step):
            remote(block, block, wb_sent, wb_sems.at[2], (s + step, f)).start()

        @pl.when(passes_down)
        def _():
            to(-2)

        @pl.when(even_up)
        def _():
            to(2)

        @pl.when(even_up if m == 1 else odd_up)
        def _():
            to(3 if m == 1 else 2)

    def slots(send, dst, sent, here, n):
        return remote(send.at[pl.ds(0, n)], dst.at[pl.ds(0, n)], sent, here, near)

    for peer in peers:
        remote(
            wa_send.at[slot_of(peer)], wa.at[slot], wa_sent, wa_sem, (s, peer)
        ).start()
    wa[slot] = wa_send[slot]

    def halo_copy(c):
        lanes = pl.ds(pl.multiple_of(c * 2048, 2048), 2048)
        return remote(
            x.at[pl.ds(96, 32), lanes], xh.at[:, lanes], halo_sent, halo_sems.at[c], (s + 1, f)
        )

    def by_slice(q):
        lanes = pl.ds(pl.multiple_of(q * 512, 512), 512)
        rows = jnp.swapaxes(xv[:, :, lanes], 0, 1)
        for k in range(4):
            x[32 * k : 32 * k + 32, lanes] = rows[k]

    with scope("slices"):

        def body(c, carry):
            x_load(c).wait()
            for q in range(4):
                by_slice(4 * c + q)

            @pl.when(jnp.logical_not(is_last))
            def _():
                halo_copy(c).start()

            return carry

        lax.fori_loop(0, 4, body, 0)

    with scope("pack_b"):
        load_fb.wait()
        for g in range(4):
            to = (g % 2) * 2 + g // 2
            for b in range(14):
                parts = [fb[t][:, 64 * g : 64 * g + 64] for t in TAPS_B[2 * b : 2 * b + 2]]
                if len(parts) < 2:
                    parts.append(jnp.zeros((64, 64), BF16))
                block = jnp.concatenate(parts, axis=1)
                for q in range(2):
                    wb_send[to, q, :, 128 * b : 128 * b + 128] = block[32 * q : 32 * q + 32]
        wb[slot] = wb_send[slot]

    def rows_of(ref, t):
        def row(r):
            return ref[:, pl.ds(pl.multiple_of(r * 128, 128), 128)]

        before = jnp.where(t > 0, row(jnp.maximum(4 * t - 1, 0)), jnp.zeros((), BF16))
        one = row(4 * t + 1)
        return (
            jnp.concatenate([before, one], 1),
            jnp.concatenate([row(4 * t), row(4 * t + 2)], 1),
            jnp.concatenate([one, row(4 * t + 3)], 1),
        )

    def taps_own(t, carry):
        cells = jnp.concatenate(rows_of(x, t), 0)
        picked = jnp.dot(cells, s1[...], preferred_element_type=F32).astype(BF16)
        lanes = pl.ds(pl.multiple_of(t * 128, 128), 128)
        for j in range(3):
            for l in range(3):
                for k in range(4):
                    piece = picked[j * 128 + k * 32 : j * 128 + k * 32 + 32, l * 128 : l * 128 + 128]
                    if k > 0:
                        at = ((k - 1) * 9 + 3 * j + l) * 32
                        v1[at : at + 32, lanes] = piece
                    if k < 2:
                        at = ((k + 1) * 9 + 3 * j + l) * 32
                        v0[at : at + 32, lanes] = piece
        return carry

    v0[864:896] = jnp.zeros((32, HALF), BF16)
    v1[864:896] = jnp.zeros((32, HALF), BF16)
    load_s1.wait()
    with scope("taps"):
        lax.fori_loop(0, 16, taps_own, 0, unroll=4)
    own_half(0).start()

    def taps_halo(q):
        cells = jnp.concatenate([c for t in range(4) for c in rows_of(xh, 4 * q + t)], 0)
        picked = jnp.dot(cells, s1[...], preferred_element_type=F32).astype(BF16)
        for t in range(4):
            lanes = pl.ds(pl.multiple_of((4 * q + t) * 128, 128), 128)
            for j in range(3):
                for l in range(3):
                    at = (3 * j + l) * 32
                    row = (3 * t + j) * 32
                    v0[at : at + 32, lanes] = picked[row : row + 32, l * 128 : l * 128 + 128]

    def sib_copy(h, c):
        return remote(part.at[h, c, 1 - core], sib.at[h, c], sib_sent, sib_sems.at[h, c], near)

    def y_copy(h, c):
        return remote(y_send.at[h, c], y_recv.at[h, c], y_sent, y_sems.at[h, c], (s, partner))

    def across(h, c):
        sib_copy(h, c).wait_recv()
        y_send[h, c] = (part[h, c, core, 1 - chip] + sib[h, c, 1 - chip]).astype(BF16)
        y_copy(h, c).start()

    def first_conv(h, v, c):
        lanes = pl.ds(pl.multiple_of(c * 512, 512), 512)
        sums = jnp.dot(wa[...].reshape(256, 896), v[:, lanes], preferred_element_type=F32)
        part[h, c] = sums.reshape(2, 2, 64, 512)
        sib_copy(h, c).start()

    def hid_copy(c):
        return remote(hid.at[2, c], hid.at[0, c], hid_sent, hid_sem, (s + 1, f))

    hid_all = remote(hid.at[2], hid.at[0], hid_sent, hid_sem, near)
    load_ba.wait()
    load_bb.wait()
    bias_a = column(biases[0])

    def finish(h, slot_h, c):
        y_copy(h, c).wait_recv()
        total = part[h, c, core, chip] + sib[h, c, chip] + y_recv[h, c].astype(F32) + bias_a
        hid[slot_h, c] = leaky(total)
        if slot_h == 2:

            @pl.when(jnp.logical_not(is_last))
            def _():
                hid_copy(c).start()

    def second_taps(i, at_i, quarters):
        def block(q):
            return hid[i, q // 4, :, 128 * (q % 4) : 128 * (q % 4) + 128]

        zero = jnp.zeros((64, 128), BF16)
        now = jnp.concatenate(
            [jnp.concatenate([block(4 * u + r) for r in range(4)], 1) for u in quarters], 0
        )
        before = jnp.concatenate(
            [
                jnp.concatenate([block(4 * u + r - 1) if 4 * u + r else zero for r in range(4)], 1)
                for u in quarters
            ],
            0,
        )
        for j, (cells, half) in enumerate(((before, 1), (now, 0), (now, 1))):
            picked = jnp.dot(cells, s2[half], preferred_element_type=F32).astype(BF16)
            for n, u in enumerate(quarters):
                for l in range(3):
                    at = (at_i * 9 + 3 * j + l) * 64
                    v2[at : at + 64, 128 * u : 128 * u + 128] = picked[
                        64 * n : 64 * n + 64, 128 * l : 128 * l + 128
                    ]

    with scope("wait_wa"):
        slots(wa_send, wa, wa_sent, wa_sem, 3).wait_recv()
    own_half(1).start()

    with scope("conv_d1"):

        def conv_d1(c, carry):
            first_conv(1, v1, c)
            return carry

        lax.fori_loop(0, 3, conv_d1, 0)

    @pl.when(is_first)
    def _():
        xh[...] = jnp.zeros(xh.shape, BF16)

    def conv_d0(c):
        with scope("halo_wait"):

            @pl.when(jnp.logical_not(is_first))
            def _():
                halo_copy(c).wait_recv()

        with scope("conv_d0"):
            taps_halo(c)
            first_conv(0, v0, c)

    def finish_d1(c):
        with scope("finish_d1"):
            finish(1, 2, c)

    def send_sums(h, c):
        with scope("across"):
            across(h, c)

    def finish_d0(c):
        with scope("finish_d0"):
            finish(0, 1, c)

    def pass_wb(m):
        with scope("pass_wb"):
            own_half(m).wait_recv()
            pass_on(m)

    def taps2(i, at_i, quarters):
        with scope("taps2"):
            second_taps(i, at_i, quarters)

    send_sums(1, 0)
    with scope("conv_d1"):
        conv_d1(3, 0)
    send_sums(1, 1)
    to_sibling(wb_send, wb, wb_sent, wb_sems.at[2]).start()
    conv_d0(0)
    send_sums(1, 2)
    conv_d0(1)
    pass_wb(0)
    conv_d0(2)
    pass_wb(1)
    finish_d1(0)
    send_sums(1, 3)
    finish_d1(1)
    send_sums(0, 0)
    conv_d0(3)
    finish_d1(2)
    send_sums(0, 1)
    finish_d1(3)
    send_sums(0, 2)
    load_s2.wait()
    v2[1728:1792] = jnp.zeros((64, QUARTER), BF16)
    taps2(2, 1, range(4))
    finish_d0(0)
    send_sums(0, 3)
    finish_d0(1)
    taps2(1, 2, (0, 1))

    @pl.when(is_first)
    def _():
        hid[0] = jnp.zeros((4, 64, 512), BF16)

    with scope("hid_wait"):

        @pl.when(jnp.logical_not(is_first))
        def _():
            hid_all.wait_recv()

    taps2(0, 0, range(4))
    with scope("wait_wb"):
        slots(wb_send, wb, wb_sent, wb_sems.at[2], 2).wait_recv()

    units = ((0, 1), (2,), (3,))

    def unit_lanes(n):
        return pl.ds(128 * units[n][0], 128 * len(units[n]))

    def sib2_copy(n):
        lanes = unit_lanes(n)
        return remote(
            part2.at[1 - core, chip, :, lanes], sib2.at[:, lanes], sib2_sent, sib2_sems.at[n], near
        )

    def z_copy(n, m):
        lanes = unit_lanes(n)
        return remote(
            z_send.at[m, :, lanes], z_recv.at[m, :, lanes], z_sent, z_sems.at[n], (s, peers[m])
        )

    for n, quarters in enumerate(units):
        lanes = unit_lanes(n)
        if n > 0:
            finish_d0(n + 1)
            taps2(1, 2, (n + 1,))
        with scope("conv2"):
            sums = jnp.dot(
                wb[...].reshape(256, 1792), v2[:, lanes], preferred_element_type=F32
            )
            part2[:, :, :, lanes] = sums.reshape(2, 2, 64, 128 * len(quarters))
            for m in range(2):
                to_core = 1 - core if m == 0 else core
                z_send[m, :, lanes] = part2[to_core, 1 - chip, :, lanes].astype(BF16)
                z_copy(n, m).start()
            sib2_copy(n).start()
    bias_b = column(biases[1])
    for n, quarters in enumerate(units):
        lanes = unit_lanes(n)
        with scope("z_wait"):
            sib2_copy(n).wait_recv()
            remote(
                z_send.at[:, :, lanes], z_recv.at[:, :, lanes], z_sent, z_sems.at[n], near
            ).wait_recv()
        far = z_recv[0, :, lanes].astype(F32) + z_recv[1, :, lanes].astype(F32)
        bias = bias_b[:, : 128 * len(quarters)]
        total = part2[core, chip, :, lanes] + sib2[:, lanes] + far + bias
        out[:, lanes] = leaky(total)

    with scope("drain"):
        slots(wa_send, wa, wa_sent, wa_sem, 3).wait_send()
        slots(wb_send, wb, wb_sent, wb_sems.at[2], 2).wait_send()

        @pl.when(passes_down)
        def _():
            slots(wb_send, wb, wb_sent, wb_sems.at[2], 1).wait_send()

        @pl.when(even_up)
        def _():
            slots(wb_send, wb, wb_sent, wb_sems.at[2], 1).wait_send()

        @pl.when(level == 2)
        def _():
            own_half(0).wait_send()

        remote(part.at[:, :, 1 - core], sib, sib_sent, sib_sems.at[0, 0], near).wait_send()
        remote(y_send, y_recv, y_sent, y_sems.at[0, 0], near).wait_send()
        remote(part2.at[1 - core, chip], sib2, sib2_sent, sib2_sems.at[0], near).wait_send()
        remote(z_send, z_recv, z_sent, z_sems.at[0], near).wait_send()

        @pl.when(jnp.logical_not(is_last))
        def _():
            remote(x.at[pl.ds(96, 32)], xh, halo_sent, halo_sems.at[0], near).wait_send()
            hid_all.wait_send()


def scattered(n_spatial, volume_in, filters_a, bias_a, filters_b, bias_b):
    vmem = pl.BlockSpec(memory_space=pltpu.VMEM)
    hbm = pl.BlockSpec(memory_space=pltpu.HBM)
    dma = pltpu.SemaphoreType.DMA

    def body(*refs):
        kernel(n_spatial, *refs)

    out = pl.pallas_call(
        body,
        out_shape=jax.ShapeDtypeStruct((64, QUARTER), BF16),
        in_specs=[hbm] * 7,
        out_specs=vmem,
        scratch_shapes=[
            pltpu.VMEM((27, 64, 128), BF16),
            pltpu.VMEM((2, 1, 64), BF16),
            pltpu.VMEM((27, 64, 256), BF16),
            pltpu.VMEM((256, 384), BF16),
            pltpu.VMEM((2, 512, 384), BF16),
            pltpu.VMEM((32, 4, ROWS * COLS), BF16),
            pltpu.VMEM((128, ROWS * COLS), BF16),
            pltpu.VMEM((32, ROWS * COLS), BF16),
            pltpu.VMEM((4, 2, 32, 896), BF16),
            pltpu.VMEM((4, 2, 32, 896), BF16),
            pltpu.VMEM((4, 2, 32, 1792), BF16),
            pltpu.VMEM((4, 2, 32, 1792), BF16),
            pltpu.VMEM((896, HALF), BF16),
            pltpu.VMEM((896, HALF), BF16),
            pltpu.VMEM((2, 4, 2, 2, 64, 512), F32),
            pltpu.VMEM((2, 4, 2, 64, 512), F32),
            pltpu.VMEM((2, 4, 64, 512), BF16),
            pltpu.VMEM((2, 4, 64, 512), BF16),
            pltpu.VMEM((3, 4, 64, 512), BF16),
            pltpu.VMEM((1792, QUARTER), BF16),
            pltpu.VMEM((2, 2, 64, 512), F32),
            pltpu.VMEM((64, 512), F32),
            pltpu.VMEM((2, 64, 512), BF16),
            pltpu.VMEM((2, 64, 512), BF16),
            dma((5,)), dma((4,)), dma((8,)), dma((4,)), dma, dma((3,)), dma((2, 4)), dma((2, 4)), dma,
            dma((3,)), dma((3,)),
        ],
        compiler_params=pltpu.CompilerParams(
            collective_id=0, has_side_effects=True, vmem_limit_bytes=52 * 1024 * 1024
        ),
        name="scattered_convs",
    )(
        *(
            pltpu.with_memory_space_constraint(a, pltpu.HBM)
            for a in (
                volume_in,
                filters_a,
                filters_b,
                bias_a.reshape(1, 64),
                bias_b.reshape(1, 64),
                jnp.asarray(pick_first(), BF16),
                jnp.asarray(pick_second(), BF16),
            )
        )
    )
    return out.reshape(64, 1, QUARTER)


def per_device(volume_in, filters_a, bias_a, filters_b, bias_b):
    n_spatial = lax.axis_size("spatial")
    own = volume_in.shape == (32, 4, ROWS * COLS) and filters_b.shape == (27, 64, 256)
    if own and n_spatial % 8 == 0:
        return scattered(n_spatial, volume_in, filters_a, bias_a, filters_b, bias_b)
    return gathered(volume_in, filters_a, bias_a, filters_b, bias_b)


def solution(mesh):
    in_specs = (
        P("filter", "spatial", None),
        P(None, "filter", None),
        P("filter"),
        P(None, "filter", None),
        P("filter"),
    )
    return jax.shard_map(
        per_device,
        mesh=mesh,
        in_specs=in_specs,
        out_specs=P("filter", "spatial", None),
        check_vma=False,
    )
```

```python
import jax
import jax.numpy as jnp
import numpy as np
from jax import lax
from jax.experimental import pallas as pl
from jax.experimental.pallas import tpu as pltpu
from jax.sharding import PartitionSpec as P

MESH = pl.DeviceIdType.MESH
ROWS = 64
COLS = 128
F32 = jnp.float32
BF16 = jnp.bfloat16


def shifted(block, axis, distance):
    devices = range(lax.axis_size(axis))
    route = [(i - distance, i) for i in devices if i - distance in devices]
    return lax.ppermute(block, axis, route)


def local_conv(block, weight, pad_rows, row_count, col_count):
    channels = block.shape[0]
    slices = block.shape[1]
    volume = block.reshape(1, channels, slices, row_count, col_count)
    kernel = weight.reshape(3, 3, 3, weight.shape[1], weight.shape[2])
    return lax.conv_general_dilated(
        volume,
        kernel,
        (2, 2, 2),
        ((0, 0), (pad_rows, pad_rows), (1, 1)),
        dimension_numbers=("NCDHW", "DHWOI", "NCDHW"),
        preferred_element_type=F32,
    )[0]


def activate(summed, bias_vec):
    summed = summed + bias_vec.astype(F32)[:, None, None, None]
    return jnp.where(summed > 0, summed, 0.2 * summed).astype(BF16)


def gathered(volume_in, filters_a, bias_a, filters_b, bias_b):
    slices = volume_in.shape[1]
    outputs = filters_a.shape[1]
    extended = jnp.concatenate([shifted(volume_in[:, -1:], "spatial", 1), volume_in], 1)
    full = lax.all_gather(extended, "filter", axis=0, tiled=True)
    hidden = activate(local_conv(full, filters_a, 1, ROWS, COLS), bias_a)
    hidden = hidden.reshape(outputs, slices // 2, ROWS // 2 * (COLS // 2))
    extended = jnp.concatenate([shifted(hidden[:, -1:], "spatial", 1), hidden], 1)
    full = lax.all_gather(extended, "filter", axis=0, tiled=True)
    out = activate(local_conv(full, filters_b, 1, ROWS // 2, COLS // 2), bias_b)
    return out.reshape(filters_b.shape[1], slices // 4, ROWS // 4 * (COLS // 4))


HALF = 2048
QUARTER = 512


def pick_first():
    s = np.zeros((256, 3, 128), np.float32)
    for l in range(3):
        for row in range(2):
            for w in range(64):
                source = 2 * w + l - 1
                if source >= 0:
                    s[row * 128 + source, l, row * 64 + w] = 1
    return s.reshape(256, 384)


def pick_second():
    s = np.zeros((2, 512, 3, 128), np.float32)
    for half in range(2):
        for l in range(3):
            for row in range(4):
                for w in range(32):
                    source = 2 * w + l - 1
                    if source >= 0:
                        s[half, row * 128 + half * 64 + source, l, row * 32 + w] = 1
    return s.reshape(2, 512, 384)


def column(row_of):
    row = lax.broadcasted_iota(jnp.int32, (64, 64), 0)
    col = lax.broadcasted_iota(jnp.int32, (64, 64), 1)
    spread = jnp.broadcast_to(row_of.astype(F32), (64, 64))
    diagonal = jnp.where(row == col, spread, 0.0).astype(BF16)
    return jnp.dot(diagonal, jnp.ones((64, 512), BF16), preferred_element_type=F32)


def leaky(u):
    return jnp.where(u > 0, u, 0.2 * u).astype(BF16)


TAPS_B = tuple(range(9)) + tuple(range(18, 27)) + tuple(range(9, 18))


def kernel(
    n_spatial, xin, fa_in, fb_in, ba_in, bb_in, s1_in, s2_in, out,
    fa, biases, fb, s1, s2, xv, x, xh, wa_send, wa, wb_send, wb, v0, v1, part, sib, y_send, y_recv, hid, v2,
    part2, sib2, z_send, z_recv,
    in_sems, x_sems, sent, halo_sems, wa_sems, wb_sems, sib_sems, y_sems, hid_sems, sib2_sems, z_sems,
):
    scope = jax.named_scope
    s = lax.axis_index("spatial")
    f = lax.axis_index("filter")
    core, chip = f % 2, f // 2
    sibling = chip * 2 + (1 - core)
    partner = (1 - chip) * 2 + core
    diagonal = (1 - chip) * 2 + (1 - core)
    slot = core * 2 + chip
    peers = (diagonal, partner, sibling)
    is_first, is_last = s == 0, s == n_spatial - 1
    is_even = s % 2 == 0
    level = (s // 2) % 4
    half = level % 2
    is_odd = s % 2 == 1
    passes_down = level > 0
    even_up = jnp.logical_and(is_even, level == 2)
    odd_up = jnp.logical_and(is_odd, level == 2)
    from_corner = jnp.logical_and(is_odd, level == 3)

    halo_sent = wa_sent = wb_sent = sib_sent = y_sent = hid_sent = sib2_sent = z_sent = sent
    for k in range(3):
        taps = pl.ds(9 * k, 9)
        pltpu.make_async_copy(fa_in.at[taps], fa.at[taps], in_sems.at[3]).start()
    load_fa = pltpu.make_async_copy(fa_in, fa, in_sems.at[3])

    def x_load(c):
        lanes = pl.ds(pl.multiple_of(c * 2048, 2048), 2048)
        return pltpu.make_async_copy(xin.at[:, :, lanes], xv.at[:, :, lanes], x_sems.at[c])

    for c in range(4):
        x_load(c).start()
    load_s1 = pltpu.make_async_copy(s1_in, s1, in_sems.at[1])
    load_fb = pltpu.make_async_copy(fb_in, fb, in_sems.at[0])
    load_ba = pltpu.make_async_copy(ba_in, biases.at[0], in_sems.at[4])
    load_bb = pltpu.make_async_copy(bb_in, biases.at[1], in_sems.at[4])
    load_s2 = pltpu.make_async_copy(s2_in, s2, in_sems.at[2])
    load_s1.start()
    load_fb.start()
    load_ba.start()
    load_bb.start()
    load_s2.start()
    barrier = pltpu.get_barrier_semaphore()
    for peer in peers:
        pl.semaphore_signal(barrier, inc=1, device_id=(s, peer), device_id_type=MESH)
    for step in (1, 2):

        @pl.when(s < n_spatial - step)
        def _():
            pl.semaphore_signal(barrier, inc=1, device_id=(s + step, f), device_id_type=MESH)

        @pl.when(s >= step)
        def _():
            pl.semaphore_signal(barrier, inc=1, device_id=(s - step, f), device_id_type=MESH)

    @pl.when(from_corner)
    def _():
        pl.semaphore_signal(barrier, inc=1, device_id=(s - 3, f), device_id_type=MESH)

    with scope("load_fa"):
        load_fa.wait()
    with scope("pack_a"):
        for g in range(4):
            to = (g % 2) * 2 + g // 2
            for b in range(7):
                parts = [fa[t][:, 32 * g : 32 * g + 32] for t in range(4 * b, min(4 * b + 4, 27))]
                if len(parts) < 4:
                    parts.append(jnp.zeros((64, 32), BF16))
                block = jnp.concatenate(parts, axis=1)
                for q in range(2):
                    wa_send[to, q, :, 128 * b : 128 * b + 128] = block[32 * q : 32 * q + 32]

    with scope("barrier"):
        neighbours = jnp.minimum(s, 2) + jnp.minimum(n_spatial - 1 - s, 2)
        pl.semaphore_wait(barrier, 3 + neighbours + jnp.where(even_up, 1, 0))

    def remote(src, dst, sent, here, target):
        return pltpu.make_async_remote_copy(
            src_ref=src, dst_ref=dst, send_sem=sent, recv_sem=here,
            device_id=target, device_id_type=MESH,
        )

    def slot_of(peer):
        return (peer % 2) * 2 + peer // 2

    near = (s, sibling)

    def to_sibling(send, dst, sent, here):
        return remote(send.at[slot_of(sibling)], dst.at[slot], sent, here, near)

    def own_half(m):
        return remote(
            wb_send.at[slot_of(peers[m]), half], wb.at[slot, half], wb_sent, wb_sems.at[m],
            (s, peers[m]),
        )

    def pass_on(m):
        block = wb.at[slot_of(peers[m]), half]

        def to(step):
            remote(block, block, wb_sent, wb_sems.at[2], (s + step, f)).start()

        @pl.when(passes_down)
        def _():
            to(-2)

        @pl.when(even_up)
        def _():
            to(2)

        @pl.when(even_up if m == 1 else odd_up)
        def _():
            to(3 if m == 1 else 2)

    def slots(send, dst, sent, here, n):
        return remote(send.at[pl.ds(0, n)], dst.at[pl.ds(0, n)], sent, here, near)

    wa_half = remote(
        wa_send.at[slot_of(partner), half], wa.at[slot, half], wa_sent, wa_sems.at[0], (s, partner)
    )

    def wa_whole(peer):
        return remote(wa_send.at[slot_of(peer)], wa.at[slot], wa_sent, wa_sems.at[1], (s, peer))

    @pl.when(core == 1)
    def _():
        wa_half.start()
        wa_whole(diagonal).start()

    @pl.when(core == 0)
    def _():
        wa_whole(partner).start()

    wa_whole(sibling).start()

    def pass_wa():
        wa_half.wait_recv()
        block = wa.at[slot_of(partner), half]

        def to(step):
            remote(block, block, wa_sent, wa_sems.at[2], (s + step, f)).start()

        @pl.when(passes_down)
        def _():
            to(-2)

        @pl.when(even_up)
        def _():
            to(2)
            to(3)

    wa[slot] = wa_send[slot]

    def halo_copy(c):
        lanes = pl.ds(pl.multiple_of(c * 2048, 2048), 2048)
        return remote(
            x.at[pl.ds(96, 32), lanes], xh.at[:, lanes], halo_sent, halo_sems.at[c], (s + 1, f)
        )

    def by_slice(q):
        lanes = pl.ds(pl.multiple_of(q * 512, 512), 512)
        rows = jnp.swapaxes(xv[:, :, lanes], 0, 1)
        for k in range(4):
            x[32 * k : 32 * k + 32, lanes] = rows[k]

    with scope("slices"):

        def body(c, carry):
            x_load(c).wait()
            for q in range(4):
                by_slice(4 * c + q)

            @pl.when(jnp.logical_not(is_last))
            def _():
                halo_copy(c).start()

            return carry

        lax.fori_loop(0, 4, body, 0)

    @pl.when(core == 0)
    def _():
        wa_whole(diagonal).start()

    with scope("pack_b"):
        load_fb.wait()
        for g in range(4):
            to = (g % 2) * 2 + g // 2
            for b in range(14):
                parts = [fb[t][:, 64 * g : 64 * g + 64] for t in TAPS_B[2 * b : 2 * b + 2]]
                if len(parts) < 2:
                    parts.append(jnp.zeros((64, 64), BF16))
                block = jnp.concatenate(parts, axis=1)
                for q in range(2):
                    wb_send[to, q, :, 128 * b : 128 * b + 128] = block[32 * q : 32 * q + 32]
        wb[slot] = wb_send[slot]

    def rows_of(ref, t):
        def row(r):
            return ref[:, pl.ds(pl.multiple_of(r * 128, 128), 128)]

        before = jnp.where(t > 0, row(jnp.maximum(4 * t - 1, 0)), jnp.zeros((), BF16))
        one = row(4 * t + 1)
        return (
            jnp.concatenate([before, one], 1),
            jnp.concatenate([row(4 * t), row(4 * t + 2)], 1),
            jnp.concatenate([one, row(4 * t + 3)], 1),
        )

    def taps_own(t, carry):
        cells = jnp.concatenate(rows_of(x, t), 0)
        picked = jnp.dot(cells, s1[...], preferred_element_type=F32).astype(BF16)
        lanes = pl.ds(pl.multiple_of(t * 128, 128), 128)
        for j in range(3):
            for l in range(3):
                for k in range(4):
                    piece = picked[j * 128 + k * 32 : j * 128 + k * 32 + 32, l * 128 : l * 128 + 128]
                    if k > 0:
                        at = ((k - 1) * 9 + 3 * j + l) * 32
                        v1[at : at + 32, lanes] = piece
                    if k < 2:
                        at = ((k + 1) * 9 + 3 * j + l) * 32
                        v0[at : at + 32, lanes] = piece
        return carry

    v0[864:896] = jnp.zeros((32, HALF), BF16)
    v1[864:896] = jnp.zeros((32, HALF), BF16)
    load_s1.wait()
    with scope("taps"):
        lax.fori_loop(0, 16, taps_own, 0, unroll=4)
    with scope("pass_wa"):
        pl.when(core == 1)(pass_wa)
    own_half(0).start()

    def taps_halo(q):
        cells = jnp.concatenate([c for t in range(4) for c in rows_of(xh, 4 * q + t)], 0)
        picked = jnp.dot(cells, s1[...], preferred_element_type=F32).astype(BF16)
        for t in range(4):
            lanes = pl.ds(pl.multiple_of((4 * q + t) * 128, 128), 128)
            for j in range(3):
                for l in range(3):
                    at = (3 * j + l) * 32
                    row = (3 * t + j) * 32
                    v0[at : at + 32, lanes] = picked[row : row + 32, l * 128 : l * 128 + 128]

    def sib_copy(h, c):
        return remote(part.at[h, c, 1 - core], sib.at[h, c], sib_sent, sib_sems.at[h, c], near)

    def y_copy(h, c):
        return remote(y_send.at[h, c], y_recv.at[h, c], y_sent, y_sems.at[h, c], (s, partner))

    def across(h, c):
        sib_copy(h, c).wait_recv()
        y_send[h, c] = (part[h, c, core, 1 - chip] + sib[h, c, 1 - chip]).astype(BF16)
        y_copy(h, c).start()

    def first_conv(h, v, c):
        lanes = pl.ds(pl.multiple_of(c * 512, 512), 512)
        sums = jnp.dot(wa[...].reshape(256, 896), v[:, lanes], preferred_element_type=F32)
        part[h, c] = sums.reshape(2, 2, 64, 512)
        sib_copy(h, c).start()

    def hid_copy(c):
        return remote(hid.at[2, c], hid.at[0, c], hid_sent, hid_sems.at[c], (s + 1, f))

    hid_all = remote(hid.at[2], hid.at[0], hid_sent, hid_sems.at[0], near)
    load_ba.wait()
    load_bb.wait()
    bias_a = column(biases[0])

    def finish(h, slot_h, c):
        y_copy(h, c).wait_recv()
        total = part[h, c, core, chip] + sib[h, c, chip] + y_recv[h, c].astype(F32) + bias_a
        hid[slot_h, c] = leaky(total)
        if slot_h == 2:

            @pl.when(jnp.logical_not(is_last))
            def _():
                hid_copy(c).start()

    def second_taps(i, at_i, quarters):
        def block(q):
            return hid[i, q // 4, :, 128 * (q % 4) : 128 * (q % 4) + 128]

        zero = jnp.zeros((64, 128), BF16)
        now = jnp.concatenate(
            [jnp.concatenate([block(4 * u + r) for r in range(4)], 1) for u in quarters], 0
        )
        before = jnp.concatenate(
            [
                jnp.concatenate([block(4 * u + r - 1) if 4 * u + r else zero for r in range(4)], 1)
                for u in quarters
            ],
            0,
        )
        for j, (cells, half) in enumerate(((before, 1), (now, 0), (now, 1))):
            picked = jnp.dot(cells, s2[half], preferred_element_type=F32).astype(BF16)
            for n, u in enumerate(quarters):
                for l in range(3):
                    at = (at_i * 9 + 3 * j + l) * 64
                    v2[at : at + 64, 128 * u : 128 * u + 128] = picked[
                        64 * n : 64 * n + 64, 128 * l : 128 * l + 128
                    ]

    with scope("wait_wa"):

        @pl.when(core == 0)
        def _():
            slots(wa_send, wa, wa_sent, wa_sems.at[1], 3).wait_recv()

        @pl.when(core == 1)
        def _():
            slots(wa_send, wa, wa_sent, wa_sems.at[1], 2).wait_recv()
            remote(wa_send.at[0, 0], wa.at[0, 0], wa_sent, wa_sems.at[2], near).wait_recv()
    own_half(1).start()

    with scope("conv_d1"):

        def conv_d1(c, carry):
            first_conv(1, v1, c)
            return carry

        lax.fori_loop(0, 3, conv_d1, 0)

    @pl.when(is_first)
    def _():
        xh[...] = jnp.zeros(xh.shape, BF16)
        hid[0] = jnp.zeros((4, 64, 512), BF16)

    def conv_d0(c):
        with scope("halo_wait"):

            @pl.when(jnp.logical_not(is_first))
            def _():
                halo_copy(c).wait_recv()

        with scope("conv_d0"):
            taps_halo(c)
            first_conv(0, v0, c)

    def finish_d1(c):
        with scope("finish_d1"):
            finish(1, 2, c)

    def send_sums(h, c):
        with scope("across"):
            across(h, c)

    def finish_d0(c):
        with scope("finish_d0"):
            finish(0, 1, c)

    def pass_wb(m):
        with scope("pass_wb"):
            own_half(m).wait_recv()
            pass_on(m)

    def taps2(i, at_i, quarters):
        with scope("taps2"):
            second_taps(i, at_i, quarters)

    send_sums(1, 0)
    with scope("conv_d1"):
        conv_d1(3, 0)
    send_sums(1, 1)
    to_sibling(wb_send, wb, wb_sent, wb_sems.at[2]).start()
    conv_d0(0)
    send_sums(1, 2)
    conv_d0(1)
    pass_wb(0)
    conv_d0(2)
    pass_wb(1)
    finish_d1(0)
    send_sums(1, 3)
    finish_d1(1)
    send_sums(0, 0)
    conv_d0(3)
    finish_d1(2)
    send_sums(0, 1)
    finish_d1(3)
    send_sums(0, 2)
    load_s2.wait()
    v2[1728:1792] = jnp.zeros((64, QUARTER), BF16)
    taps2(2, 1, range(4))
    finish_d0(0)
    send_sums(0, 3)

    def halo_taps(quarters):
        with scope("hid_wait"):

            @pl.when(jnp.logical_not(is_first))
            def _():
                for c in quarters:
                    hid_copy(c).wait_recv()

        taps2(0, 0, quarters)

    halo_taps((0, 1))
    finish_d0(1)
    taps2(1, 2, (0, 1))
    with scope("wait_wb"):
        slots(wb_send, wb, wb_sent, wb_sems.at[2], 2).wait_recv()

    units = ((0, 1), (2,), (3,))

    def unit_lanes(n):
        return pl.ds(128 * units[n][0], 128 * len(units[n]))

    def sib2_copy(n):
        lanes = unit_lanes(n)
        return remote(
            part2.at[1 - core, chip, :, lanes], sib2.at[:, lanes], sib2_sent, sib2_sems.at[n], near
        )

    def z_copy(n, m):
        lanes = unit_lanes(n)
        return remote(
            z_send.at[m, :, lanes], z_recv.at[m, :, lanes], z_sent, z_sems.at[n], (s, peers[m])
        )

    for n, quarters in enumerate(units):
        lanes = unit_lanes(n)
        if n > 0:
            halo_taps((n + 1,))
            finish_d0(n + 1)
            taps2(1, 2, (n + 1,))
        with scope("conv2"):
            sums = jnp.dot(
                wb[...].reshape(256, 1792), v2[:, lanes], preferred_element_type=F32
            )
            part2[:, :, :, lanes] = sums.reshape(2, 2, 64, 128 * len(quarters))
            for m in range(2):
                to_core = 1 - core if m == 0 else core
                z_send[m, :, lanes] = part2[to_core, 1 - chip, :, lanes].astype(BF16)
                z_copy(n, m).start()
            sib2_copy(n).start()
    bias_b = column(biases[1])
    for n, quarters in enumerate(units):
        lanes = unit_lanes(n)
        with scope("z_wait"):
            sib2_copy(n).wait_recv()
            remote(
                z_send.at[:, :, lanes], z_recv.at[:, :, lanes], z_sent, z_sems.at[n], near
            ).wait_recv()
        far = z_recv[0, :, lanes].astype(F32) + z_recv[1, :, lanes].astype(F32)
        bias = bias_b[:, : 128 * len(quarters)]
        total = part2[core, chip, :, lanes] + sib2[:, lanes] + far + bias
        out[:, lanes] = leaky(total)

    with scope("drain"):
        slots(wa_send, wa, wa_sent, wa_sems.at[1], 2).wait_send()

        @pl.when(core == 0)
        def _():
            slots(wa_send, wa, wa_sent, wa_sems.at[1], 1).wait_send()

        @pl.when(core == 1)
        def _():
            wa_half.wait_send()

        @pl.when(jnp.logical_and(core == 1, passes_down))
        def _():
            wa_half.wait_send()

        @pl.when(jnp.logical_and(core == 1, even_up))
        def _():
            slots(wa_send, wa, wa_sent, wa_sems.at[1], 1).wait_send()

        slots(wb_send, wb, wb_sent, wb_sems.at[2], 2).wait_send()

        @pl.when(passes_down)
        def _():
            slots(wb_send, wb, wb_sent, wb_sems.at[2], 1).wait_send()

        @pl.when(even_up)
        def _():
            slots(wb_send, wb, wb_sent, wb_sems.at[2], 1).wait_send()

        @pl.when(level == 2)
        def _():
            own_half(0).wait_send()

        remote(part.at[:, :, 1 - core], sib, sib_sent, sib_sems.at[0, 0], near).wait_send()
        remote(y_send, y_recv, y_sent, y_sems.at[0, 0], near).wait_send()
        remote(part2.at[1 - core, chip], sib2, sib2_sent, sib2_sems.at[0], near).wait_send()
        remote(z_send, z_recv, z_sent, z_sems.at[0], near).wait_send()

        @pl.when(jnp.logical_not(is_last))
        def _():
            remote(x.at[pl.ds(96, 32)], xh, halo_sent, halo_sems.at[0], near).wait_send()
            hid_all.wait_send()


def scattered(n_spatial, volume_in, filters_a, bias_a, filters_b, bias_b):
    vmem = pl.BlockSpec(memory_space=pltpu.VMEM)
    hbm = pl.BlockSpec(memory_space=pltpu.HBM)
    dma = pltpu.SemaphoreType.DMA

    def body(*refs):
        kernel(n_spatial, *refs)

    out = pl.pallas_call(
        body,
        out_shape=jax.ShapeDtypeStruct((64, QUARTER), BF16),
        in_specs=[hbm] * 7,
        out_specs=vmem,
        scratch_shapes=[
            pltpu.VMEM((27, 64, 128), BF16),
            pltpu.VMEM((2, 1, 64), BF16),
            pltpu.VMEM((27, 64, 256), BF16),
            pltpu.VMEM((256, 384), BF16),
            pltpu.VMEM((2, 512, 384), BF16),
            pltpu.VMEM((32, 4, ROWS * COLS), BF16),
            pltpu.VMEM((128, ROWS * COLS), BF16),
            pltpu.VMEM((32, ROWS * COLS), BF16),
            pltpu.VMEM((4, 2, 32, 896), BF16),
            pltpu.VMEM((4, 2, 32, 896), BF16),
            pltpu.VMEM((4, 2, 32, 1792), BF16),
            pltpu.VMEM((4, 2, 32, 1792), BF16),
            pltpu.VMEM((896, HALF), BF16),
            pltpu.VMEM((896, HALF), BF16),
            pltpu.VMEM((2, 4, 2, 2, 64, 512), F32),
            pltpu.VMEM((2, 4, 2, 64, 512), F32),
            pltpu.VMEM((2, 4, 64, 512), BF16),
            pltpu.VMEM((2, 4, 64, 512), BF16),
            pltpu.VMEM((3, 4, 64, 512), BF16),
            pltpu.VMEM((1792, QUARTER), BF16),
            pltpu.VMEM((2, 2, 64, 512), F32),
            pltpu.VMEM((64, 512), F32),
            pltpu.VMEM((2, 64, 512), BF16),
            pltpu.VMEM((2, 64, 512), BF16),
            dma((5,)), dma((4,)), dma, dma((4,)), dma((3,)), dma((3,)), dma((2, 4)), dma((2, 4)), dma((4,)),
            dma((3,)), dma((3,)),
        ],
        compiler_params=pltpu.CompilerParams(
            collective_id=0, has_side_effects=True, vmem_limit_bytes=52 * 1024 * 1024
        ),
        name="scattered_convs",
    )(
        *(
            pltpu.with_memory_space_constraint(a, pltpu.HBM)
            for a in (
                volume_in,
                filters_a,
                filters_b,
                bias_a.reshape(1, 64),
                bias_b.reshape(1, 64),
                jnp.asarray(pick_first(), BF16),
                jnp.asarray(pick_second(), BF16),
            )
        )
    )
    return out.reshape(64, 1, QUARTER)


def per_device(volume_in, filters_a, bias_a, filters_b, bias_b):
    n_spatial = lax.axis_size("spatial")
    own = volume_in.shape == (32, 4, ROWS * COLS) and filters_b.shape == (27, 64, 256)
    if own and n_spatial % 8 == 0:
        return scattered(n_spatial, volume_in, filters_a, bias_a, filters_b, bias_b)
    return gathered(volume_in, filters_a, bias_a, filters_b, bias_b)


def solution(mesh):
    in_specs = (
        P("filter", "spatial", None),
        P(None, "filter", None),
        P("filter"),
        P(None, "filter", None),
        P("filter"),
    )
    return jax.shard_map(
        per_device,
        mesh=mesh,
        in_specs=in_specs,
        out_specs=P("filter", "spatial", None),
        check_vma=False,
    )
```

```python
import jax
import jax.numpy as jnp
import numpy as np
from jax import lax
from jax.experimental import pallas as pl
from jax.experimental.pallas import tpu as pltpu
from jax.sharding import PartitionSpec as P

MESH = pl.DeviceIdType.MESH
ROWS = 64
COLS = 128
F32 = jnp.float32
BF16 = jnp.bfloat16


def shifted(block, axis, distance):
    devices = range(lax.axis_size(axis))
    route = [(i - distance, i) for i in devices if i - distance in devices]
    return lax.ppermute(block, axis, route)


def local_conv(block, weight, pad_rows, row_count, col_count):
    channels = block.shape[0]
    slices = block.shape[1]
    volume = block.reshape(1, channels, slices, row_count, col_count)
    kernel = weight.reshape(3, 3, 3, weight.shape[1], weight.shape[2])
    return lax.conv_general_dilated(
        volume,
        kernel,
        (2, 2, 2),
        ((0, 0), (pad_rows, pad_rows), (1, 1)),
        dimension_numbers=("NCDHW", "DHWOI", "NCDHW"),
        preferred_element_type=F32,
    )[0]


def activate(summed, bias_vec):
    summed = summed + bias_vec.astype(F32)[:, None, None, None]
    return jnp.where(summed > 0, summed, 0.2 * summed).astype(BF16)


def gathered(volume_in, filters_a, bias_a, filters_b, bias_b):
    slices = volume_in.shape[1]
    outputs = filters_a.shape[1]
    extended = jnp.concatenate([shifted(volume_in[:, -1:], "spatial", 1), volume_in], 1)
    full = lax.all_gather(extended, "filter", axis=0, tiled=True)
    hidden = activate(local_conv(full, filters_a, 1, ROWS, COLS), bias_a)
    hidden = hidden.reshape(outputs, slices // 2, ROWS // 2 * (COLS // 2))
    extended = jnp.concatenate([shifted(hidden[:, -1:], "spatial", 1), hidden], 1)
    full = lax.all_gather(extended, "filter", axis=0, tiled=True)
    out = activate(local_conv(full, filters_b, 1, ROWS // 2, COLS // 2), bias_b)
    return out.reshape(filters_b.shape[1], slices // 4, ROWS // 4 * (COLS // 4))


HALF = 2048
QUARTER = 512


def pick_first():
    s = np.zeros((256, 3, 128), np.float32)
    for l in range(3):
        for row in range(2):
            for w in range(64):
                source = 2 * w + l - 1
                if source >= 0:
                    s[row * 128 + source, l, row * 64 + w] = 1
    return s.reshape(256, 384)


def pick_second():
    s = np.zeros((2, 512, 3, 128), np.float32)
    for half in range(2):
        for l in range(3):
            for row in range(4):
                for w in range(32):
                    source = 2 * w + l - 1
                    if source >= 0:
                        s[half, row * 128 + half * 64 + source, l, row * 32 + w] = 1
    return s.reshape(2, 512, 384)


def column(row_of):
    row = lax.broadcasted_iota(jnp.int32, (64, 64), 0)
    col = lax.broadcasted_iota(jnp.int32, (64, 64), 1)
    spread = jnp.broadcast_to(row_of.astype(F32), (64, 64))
    diagonal = jnp.where(row == col, spread, 0.0).astype(BF16)
    return jnp.dot(diagonal, jnp.ones((64, 512), BF16), preferred_element_type=F32)


def leaky(u):
    return jnp.where(u > 0, u, 0.2 * u).astype(BF16)


TAPS_B = tuple(range(9)) + tuple(range(18, 27)) + tuple(range(9, 18))


def kernel(
    n_spatial, xin, fa_in, fb_in, ba_in, bb_in, s1_in, s2_in, out,
    fa, biases, fb, s1, s2, xv, x, xh, wa_send, wa, wb_send, wb, v0, v1, part, sib, y_send, y_recv, hid, v2,
    part2, sib2, z_send, z_recv,
    in_sems, x_sems, sent, halo_sems, wa_sems, wb_sems, sib_sems, y_sems, hid_sems, sib2_sems, z_sems,
):
    scope = jax.named_scope
    s = lax.axis_index("spatial")
    f = lax.axis_index("filter")
    core, chip = f % 2, f // 2
    sibling = chip * 2 + (1 - core)
    partner = (1 - chip) * 2 + core
    diagonal = (1 - chip) * 2 + (1 - core)
    slot = core * 2 + chip
    peers = (diagonal, partner, sibling)
    is_first, is_last = s == 0, s == n_spatial - 1
    is_even = s % 2 == 0
    level = (s // 2) % 4
    half = level % 2
    is_odd = s % 2 == 1
    passes_down = level > 0
    even_up = jnp.logical_and(is_even, level == 2)
    odd_up = jnp.logical_and(is_odd, level == 2)
    from_corner = jnp.logical_and(is_odd, level == 3)

    halo_sent = wa_sent = wb_sent = sib_sent = y_sent = hid_sent = sib2_sent = z_sent = sent
    for k in range(3):
        taps = pl.ds(9 * k, 9)
        pltpu.make_async_copy(fa_in.at[taps], fa.at[taps], in_sems.at[3]).start()
    load_fa = pltpu.make_async_copy(fa_in, fa, in_sems.at[3])

    def x_load(c):
        lanes = pl.ds(pl.multiple_of(c * 2048, 2048), 2048)
        return pltpu.make_async_copy(xin.at[:, :, lanes], xv.at[:, :, lanes], x_sems.at[c])

    for c in range(4):
        x_load(c).start()
    load_s1 = pltpu.make_async_copy(s1_in, s1, in_sems.at[1])
    load_fb = pltpu.make_async_copy(fb_in, fb, in_sems.at[0])
    load_ba = pltpu.make_async_copy(ba_in, biases.at[0], in_sems.at[4])
    load_bb = pltpu.make_async_copy(bb_in, biases.at[1], in_sems.at[4])
    load_s2 = pltpu.make_async_copy(s2_in, s2, in_sems.at[2])
    load_s1.start()
    load_fb.start()
    load_ba.start()
    load_bb.start()
    load_s2.start()
    barrier = pltpu.get_barrier_semaphore()
    for peer in peers:
        pl.semaphore_signal(barrier, inc=1, device_id=(s, peer), device_id_type=MESH)
    for step in (1, 2):

        @pl.when(s < n_spatial - step)
        def _():
            pl.semaphore_signal(barrier, inc=1, device_id=(s + step, f), device_id_type=MESH)

        @pl.when(s >= step)
        def _():
            pl.semaphore_signal(barrier, inc=1, device_id=(s - step, f), device_id_type=MESH)

    @pl.when(from_corner)
    def _():
        pl.semaphore_signal(barrier, inc=1, device_id=(s - 3, f), device_id_type=MESH)

    def pack_a(g):
        to = (g % 2) * 2 + g // 2
        for b in range(7):
            parts = [fa[t][:, 32 * g : 32 * g + 32] for t in range(4 * b, min(4 * b + 4, 27))]
            if len(parts) < 4:
                parts.append(jnp.zeros((64, 32), BF16))
            block = jnp.concatenate(parts, axis=1)
            for q in range(2):
                wa_send[to, q, :, 128 * b : 128 * b + 128] = block[32 * q : 32 * q + 32]

    def pack_blocks(of_chip):
        for k in range(2):

            @pl.when(of_chip == k)
            def _():
                pack_a(2 * k)
                pack_a(2 * k + 1)

    with scope("load_fa"):
        load_fa.wait()
    with scope("pack_a"):
        pack_blocks(1 - chip)

    with scope("barrier"):
        neighbours = jnp.minimum(s, 2) + jnp.minimum(n_spatial - 1 - s, 2)
        pl.semaphore_wait(barrier, 3 + neighbours + jnp.where(even_up, 1, 0))

    def remote(src, dst, sent, here, target):
        return pltpu.make_async_remote_copy(
            src_ref=src, dst_ref=dst, send_sem=sent, recv_sem=here,
            device_id=target, device_id_type=MESH,
        )

    def slot_of(peer):
        return (peer % 2) * 2 + peer // 2

    near = (s, sibling)

    def to_sibling(send, dst, sent, here):
        return remote(send.at[slot_of(sibling)], dst.at[slot], sent, here, near)

    def own_half(m):
        return remote(
            wb_send.at[slot_of(peers[m]), half], wb.at[slot, half], wb_sent, wb_sems.at[m],
            (s, peers[m]),
        )

    def pass_on(m):
        block = wb.at[slot_of(peers[m]), half]

        def to(step):
            remote(block, block, wb_sent, wb_sems.at[2], (s + step, f)).start()

        @pl.when(passes_down)
        def _():
            to(-2)

        @pl.when(even_up)
        def _():
            to(2)

        @pl.when(even_up if m == 1 else odd_up)
        def _():
            to(3 if m == 1 else 2)

    def slots(send, dst, sent, here, n):
        return remote(send.at[pl.ds(0, n)], dst.at[pl.ds(0, n)], sent, here, near)

    wa_half = remote(
        wa_send.at[slot_of(partner), half], wa.at[slot, half], wa_sent, wa_sems.at[0], (s, partner)
    )

    def wa_whole(peer):
        return remote(wa_send.at[slot_of(peer)], wa.at[slot], wa_sent, wa_sems.at[1], (s, peer))

    @pl.when(core == 1)
    def _():
        wa_half.start()
        wa_whole(diagonal).start()

    @pl.when(core == 0)
    def _():
        wa_whole(partner).start()

    with scope("pack_a"):
        pack_blocks(chip)
    wa_whole(sibling).start()

    def pass_wa():
        wa_half.wait_recv()
        block = wa.at[slot_of(partner), half]

        def to(step):
            remote(block, block, wa_sent, wa_sems.at[2], (s + step, f)).start()

        @pl.when(passes_down)
        def _():
            to(-2)

        @pl.when(even_up)
        def _():
            to(2)
            to(3)

    wa[slot] = wa_send[slot]

    def halo_copy(c):
        lanes = pl.ds(pl.multiple_of(c * 2048, 2048), 2048)
        return remote(
            x.at[pl.ds(96, 32), lanes], xh.at[:, lanes], halo_sent, halo_sems.at[c], (s + 1, f)
        )

    def by_slice(q):
        lanes = pl.ds(pl.multiple_of(q * 512, 512), 512)
        rows = jnp.swapaxes(xv[:, :, lanes], 0, 1)
        for k in range(4):
            x[32 * k : 32 * k + 32, lanes] = rows[k]

    with scope("slices"):

        def body(c, carry):
            x_load(c).wait()
            for q in range(4):
                by_slice(4 * c + q)

            @pl.when(jnp.logical_not(is_last))
            def _():
                halo_copy(c).start()

            return carry

        lax.fori_loop(0, 4, body, 0)

    @pl.when(core == 0)
    def _():
        wa_whole(diagonal).start()

    with scope("pack_b"):
        load_fb.wait()
        for g in range(4):
            to = (g % 2) * 2 + g // 2
            for b in range(14):
                parts = [fb[t][:, 64 * g : 64 * g + 64] for t in TAPS_B[2 * b : 2 * b + 2]]
                if len(parts) < 2:
                    parts.append(jnp.zeros((64, 64), BF16))
                block = jnp.concatenate(parts, axis=1)
                for q in range(2):
                    wb_send[to, q, :, 128 * b : 128 * b + 128] = block[32 * q : 32 * q + 32]
        wb[slot] = wb_send[slot]

    def rows_of(ref, t):
        def row(r):
            return ref[:, pl.ds(pl.multiple_of(r * 128, 128), 128)]

        before = jnp.where(t > 0, row(jnp.maximum(4 * t - 1, 0)), jnp.zeros((), BF16))
        one = row(4 * t + 1)
        return (
            jnp.concatenate([before, one], 1),
            jnp.concatenate([row(4 * t), row(4 * t + 2)], 1),
            jnp.concatenate([one, row(4 * t + 3)], 1),
        )

    def taps_own(t, carry):
        cells = jnp.concatenate(rows_of(x, t), 0)
        picked = jnp.dot(cells, s1[...], preferred_element_type=F32).astype(BF16)
        lanes = pl.ds(pl.multiple_of(t * 128, 128), 128)
        for j in range(3):
            for l in range(3):
                for k in range(4):
                    piece = picked[j * 128 + k * 32 : j * 128 + k * 32 + 32, l * 128 : l * 128 + 128]
                    if k > 0:
                        at = ((k - 1) * 9 + 3 * j + l) * 32
                        v1[at : at + 32, lanes] = piece
                    if k < 2:
                        at = ((k + 1) * 9 + 3 * j + l) * 32
                        v0[at : at + 32, lanes] = piece
        return carry

    v0[864:896] = jnp.zeros((32, HALF), BF16)
    v1[864:896] = jnp.zeros((32, HALF), BF16)
    load_s1.wait()
    with scope("taps"):
        lax.fori_loop(0, 16, taps_own, 0, unroll=4)
    with scope("pass_wa"):
        pl.when(core == 1)(pass_wa)
    own_half(0).start()

    def taps_halo(q):
        cells = jnp.concatenate([c for t in range(4) for c in rows_of(xh, 4 * q + t)], 0)
        picked = jnp.dot(cells, s1[...], preferred_element_type=F32).astype(BF16)
        for t in range(4):
            lanes = pl.ds(pl.multiple_of((4 * q + t) * 128, 128), 128)
            for j in range(3):
                for l in range(3):
                    at = (3 * j + l) * 32
                    row = (3 * t + j) * 32
                    v0[at : at + 32, lanes] = picked[row : row + 32, l * 128 : l * 128 + 128]

    def sib_copy(h, c):
        return remote(part.at[h, c, 1 - core], sib.at[h, c], sib_sent, sib_sems.at[h, c], near)

    def y_copy(h, c):
        return remote(y_send.at[h, c], y_recv.at[h, c], y_sent, y_sems.at[h, c], (s, partner))

    def across(h, c):
        sib_copy(h, c).wait_recv()
        y_send[h, c] = (part[h, c, core, 1 - chip] + sib[h, c, 1 - chip]).astype(BF16)
        y_copy(h, c).start()

    def first_conv(h, v, c):
        lanes = pl.ds(pl.multiple_of(c * 512, 512), 512)
        sums = jnp.dot(wa[...].reshape(256, 896), v[:, lanes], preferred_element_type=F32)
        part[h, c] = sums.reshape(2, 2, 64, 512)
        sib_copy(h, c).start()

    def hid_copy(c):
        return remote(hid.at[2, c], hid.at[0, c], hid_sent, hid_sems.at[c], (s + 1, f))

    hid_all = remote(hid.at[2], hid.at[0], hid_sent, hid_sems.at[0], near)
    load_ba.wait()
    load_bb.wait()
    bias_a = column(biases[0])

    def finish(h, slot_h, c):
        y_copy(h, c).wait_recv()
        total = part[h, c, core, chip] + sib[h, c, chip] + y_recv[h, c].astype(F32) + bias_a
        hid[slot_h, c] = leaky(total)
        if slot_h == 2:

            @pl.when(jnp.logical_not(is_last))
            def _():
                hid_copy(c).start()

    def second_taps(i, at_i, quarters):
        def block(q):
            return hid[i, q // 4, :, 128 * (q % 4) : 128 * (q % 4) + 128]

        zero = jnp.zeros((64, 128), BF16)
        now = jnp.concatenate(
            [jnp.concatenate([block(4 * u + r) for r in range(4)], 1) for u in quarters], 0
        )
        before = jnp.concatenate(
            [
                jnp.concatenate([block(4 * u + r - 1) if 4 * u + r else zero for r in range(4)], 1)
                for u in quarters
            ],
            0,
        )
        for j, (cells, half) in enumerate(((before, 1), (now, 0), (now, 1))):
            picked = jnp.dot(cells, s2[half], preferred_element_type=F32).astype(BF16)
            for n, u in enumerate(quarters):
                for l in range(3):
                    at = (at_i * 9 + 3 * j + l) * 64
                    v2[at : at + 64, 128 * u : 128 * u + 128] = picked[
                        64 * n : 64 * n + 64, 128 * l : 128 * l + 128
                    ]

    with scope("wait_wa"):

        @pl.when(core == 0)
        def _():
            slots(wa_send, wa, wa_sent, wa_sems.at[1], 3).wait_recv()

        @pl.when(core == 1)
        def _():
            slots(wa_send, wa, wa_sent, wa_sems.at[1], 2).wait_recv()
            remote(wa_send.at[0, 0], wa.at[0, 0], wa_sent, wa_sems.at[2], near).wait_recv()
    pl.when(core == 0)(own_half(1).start)

    with scope("conv_d1"):

        def conv_d1(c, carry):
            first_conv(1, v1, c)
            return carry

        def conv_and_send(c, carry):
            first_conv(1, v1, c)
            across(1, c)
            return carry

        def send_one(c, carry):
            across(1, c)
            return carry

        @pl.when(core == 0)
        def _():
            lax.fori_loop(0, 4, conv_d1, 0)
            lax.fori_loop(0, 3, send_one, 0)

        @pl.when(core == 1)
        def _():
            conv_and_send(0, 0)
            own_half(1).start()
            lax.fori_loop(1, 3, conv_and_send, 0)
            conv_d1(3, 0)

    @pl.when(is_first)
    def _():
        xh[...] = jnp.zeros(xh.shape, BF16)
        hid[0] = jnp.zeros((4, 64, 512), BF16)

    def conv_d0(c):
        with scope("halo_wait"):

            @pl.when(jnp.logical_not(is_first))
            def _():
                halo_copy(c).wait_recv()

        with scope("conv_d0"):
            taps_halo(c)
            first_conv(0, v0, c)

    def finish_d1(c):
        with scope("finish_d1"):
            finish(1, 2, c)

    def send_sums(h, c):
        with scope("across"):
            across(h, c)

    def finish_d0(c):
        with scope("finish_d0"):
            finish(0, 1, c)

    def pass_wb(m):
        with scope("pass_wb"):
            own_half(m).wait_recv()
            pass_on(m)

    def taps2(i, at_i, quarters):
        with scope("taps2"):
            second_taps(i, at_i, quarters)

    to_sibling(wb_send, wb, wb_sent, wb_sems.at[2]).start()
    conv_d0(0)
    conv_d0(1)
    pass_wb(0)
    conv_d0(2)
    pass_wb(1)
    finish_d1(0)
    send_sums(1, 3)
    finish_d1(1)
    send_sums(0, 0)
    conv_d0(3)
    finish_d1(2)
    send_sums(0, 1)
    finish_d1(3)
    send_sums(0, 2)
    load_s2.wait()
    v2[1728:1792] = jnp.zeros((64, QUARTER), BF16)
    taps2(2, 1, range(4))
    finish_d0(0)
    send_sums(0, 3)

    def halo_taps(quarters):
        with scope("hid_wait"):

            @pl.when(jnp.logical_not(is_first))
            def _():
                for c in quarters:
                    hid_copy(c).wait_recv()

        taps2(0, 0, quarters)

    halo_taps((0, 1))
    finish_d0(1)
    taps2(1, 2, (0, 1))
    with scope("wait_wb"):
        slots(wb_send, wb, wb_sent, wb_sems.at[2], 2).wait_recv()

    units = ((0, 1), (2,), (3,))

    def unit_lanes(n):
        return pl.ds(128 * units[n][0], 128 * len(units[n]))

    def sib2_copy(n):
        lanes = unit_lanes(n)
        return remote(
            part2.at[1 - core, chip, :, lanes], sib2.at[:, lanes], sib2_sent, sib2_sems.at[n], near
        )

    def z_copy(n, k):
        lanes = unit_lanes(n)
        return remote(
            z_send.at[k, :, lanes], z_recv.at[core, :, lanes], z_sent, z_sems.at[n],
            (s, (1 - chip) * 2 + k),
        )

    def conv2(n, rows, at):
        lanes = unit_lanes(n)
        sums = jnp.dot(
            wb[:, :, :, at : at + rows].reshape(256, rows),
            v2[at : at + rows, lanes],
            preferred_element_type=F32,
        )
        return sums.reshape(2, 2, 64, 128 * len(units[n]))

    for n, quarters in enumerate(units):
        lanes = unit_lanes(n)
        if n > 0:
            halo_taps((n + 1,))
            if n == 2:
                with scope("conv2_sides"):
                    part2[:, :, :, lanes] = conv2(n, 1152, 0)
            finish_d0(n + 1)
            taps2(1, 2, (n + 1,))
        with scope("conv2"):
            if n == 2:
                part2[:, :, :, lanes] = part2[:, :, :, lanes] + conv2(n, 640, 1152)
            else:
                part2[:, :, :, lanes] = conv2(n, 1792, 0)
            for k in range(2):
                z_send[k, :, lanes] = part2[k, 1 - chip, :, lanes].astype(BF16)
                z_copy(n, k).start()
            sib2_copy(n).start()
    bias_b = column(biases[1])
    for n, quarters in enumerate(units):
        lanes = unit_lanes(n)
        with scope("z_wait"):
            sib2_copy(n).wait_recv()
            remote(
                z_send.at[:, :, lanes], z_recv.at[:, :, lanes], z_sent, z_sems.at[n], near
            ).wait_recv()
        far = z_recv[0, :, lanes].astype(F32) + z_recv[1, :, lanes].astype(F32)
        bias = bias_b[:, : 128 * len(quarters)]
        total = part2[core, chip, :, lanes] + sib2[:, lanes] + far + bias
        out[:, lanes] = leaky(total)

    with scope("drain"):
        slots(wa_send, wa, wa_sent, wa_sems.at[1], 2).wait_send()

        @pl.when(core == 0)
        def _():
            slots(wa_send, wa, wa_sent, wa_sems.at[1], 1).wait_send()

        @pl.when(core == 1)
        def _():
            wa_half.wait_send()

        @pl.when(jnp.logical_and(core == 1, passes_down))
        def _():
            wa_half.wait_send()

        @pl.when(jnp.logical_and(core == 1, even_up))
        def _():
            slots(wa_send, wa, wa_sent, wa_sems.at[1], 1).wait_send()

        slots(wb_send, wb, wb_sent, wb_sems.at[2], 2).wait_send()

        @pl.when(passes_down)
        def _():
            slots(wb_send, wb, wb_sent, wb_sems.at[2], 1).wait_send()

        @pl.when(even_up)
        def _():
            slots(wb_send, wb, wb_sent, wb_sems.at[2], 1).wait_send()

        @pl.when(level == 2)
        def _():
            own_half(0).wait_send()

        remote(part.at[:, :, 1 - core], sib, sib_sent, sib_sems.at[0, 0], near).wait_send()
        remote(y_send, y_recv, y_sent, y_sems.at[0, 0], near).wait_send()
        remote(part2.at[1 - core, chip], sib2, sib2_sent, sib2_sems.at[0], near).wait_send()
        remote(z_send, z_recv, z_sent, z_sems.at[0], near).wait_send()

        @pl.when(jnp.logical_not(is_last))
        def _():
            remote(x.at[pl.ds(96, 32)], xh, halo_sent, halo_sems.at[0], near).wait_send()
            hid_all.wait_send()


def scattered(n_spatial, volume_in, filters_a, bias_a, filters_b, bias_b):
    vmem = pl.BlockSpec(memory_space=pltpu.VMEM)
    hbm = pl.BlockSpec(memory_space=pltpu.HBM)
    dma = pltpu.SemaphoreType.DMA

    def body(*refs):
        kernel(n_spatial, *refs)

    out = pl.pallas_call(
        body,
        out_shape=jax.ShapeDtypeStruct((64, QUARTER), BF16),
        in_specs=[hbm] * 7,
        out_specs=vmem,
        scratch_shapes=[
            pltpu.VMEM((27, 64, 128), BF16),
            pltpu.VMEM((2, 1, 64), BF16),
            pltpu.VMEM((27, 64, 256), BF16),
            pltpu.VMEM((256, 384), BF16),
            pltpu.VMEM((2, 512, 384), BF16),
            pltpu.VMEM((32, 4, ROWS * COLS), BF16),
            pltpu.VMEM((128, ROWS * COLS), BF16),
            pltpu.VMEM((32, ROWS * COLS), BF16),
            pltpu.VMEM((4, 2, 32, 896), BF16),
            pltpu.VMEM((4, 2, 32, 896), BF16),
            pltpu.VMEM((4, 2, 32, 1792), BF16),
            pltpu.VMEM((4, 2, 32, 1792), BF16),
            pltpu.VMEM((896, HALF), BF16),
            pltpu.VMEM((896, HALF), BF16),
            pltpu.VMEM((2, 4, 2, 2, 64, 512), F32),
            pltpu.VMEM((2, 4, 2, 64, 512), F32),
            pltpu.VMEM((2, 4, 64, 512), BF16),
            pltpu.VMEM((2, 4, 64, 512), BF16),
            pltpu.VMEM((3, 4, 64, 512), BF16),
            pltpu.VMEM((1792, QUARTER), BF16),
            pltpu.VMEM((2, 2, 64, 512), F32),
            pltpu.VMEM((64, 512), F32),
            pltpu.VMEM((2, 64, 512), BF16),
            pltpu.VMEM((2, 64, 512), BF16),
            dma((5,)), dma((4,)), dma, dma((4,)), dma((3,)), dma((3,)), dma((2, 4)), dma((2, 4)), dma((4,)),
            dma((3,)), dma((3,)),
        ],
        compiler_params=pltpu.CompilerParams(
            collective_id=0, has_side_effects=True, vmem_limit_bytes=52 * 1024 * 1024
        ),
        name="scattered_convs",
    )(
        *(
            pltpu.with_memory_space_constraint(a, pltpu.HBM)
            for a in (
                volume_in,
                filters_a,
                filters_b,
                bias_a.reshape(1, 64),
                bias_b.reshape(1, 64),
                jnp.asarray(pick_first(), BF16),
                jnp.asarray(pick_second(), BF16),
            )
        )
    )
    return out.reshape(64, 1, QUARTER)


def per_device(volume_in, filters_a, bias_a, filters_b, bias_b):
    n_spatial = lax.axis_size("spatial")
    own = volume_in.shape == (32, 4, ROWS * COLS) and filters_b.shape == (27, 64, 256)
    if own and n_spatial % 8 == 0:
        return scattered(n_spatial, volume_in, filters_a, bias_a, filters_b, bias_b)
    return gathered(volume_in, filters_a, bias_a, filters_b, bias_b)


def solution(mesh):
    in_specs = (
        P("filter", "spatial", None),
        P(None, "filter", None),
        P("filter"),
        P(None, "filter", None),
        P("filter"),
    )
    return jax.shard_map(
        per_device,
        mesh=mesh,
        in_specs=in_specs,
        out_specs=P("filter", "spatial", None),
        check_vma=False,
    )
```

```python
import jax
import jax.numpy as jnp
import numpy as np
from jax import lax
from jax.experimental import pallas as pl
from jax.experimental.pallas import tpu as pltpu
from jax.sharding import PartitionSpec as P

MESH = pl.DeviceIdType.MESH
ROWS = 64
COLS = 128
F32 = jnp.float32
BF16 = jnp.bfloat16


def shifted(block, axis, distance):
    devices = range(lax.axis_size(axis))
    route = [(i - distance, i) for i in devices if i - distance in devices]
    return lax.ppermute(block, axis, route)


def local_conv(block, weight, pad_rows, row_count, col_count):
    channels = block.shape[0]
    slices = block.shape[1]
    volume = block.reshape(1, channels, slices, row_count, col_count)
    kernel = weight.reshape(3, 3, 3, weight.shape[1], weight.shape[2])
    return lax.conv_general_dilated(
        volume,
        kernel,
        (2, 2, 2),
        ((0, 0), (pad_rows, pad_rows), (1, 1)),
        dimension_numbers=("NCDHW", "DHWOI", "NCDHW"),
        preferred_element_type=F32,
    )[0]


def activate(summed, bias_vec):
    summed = summed + bias_vec.astype(F32)[:, None, None, None]
    return jnp.where(summed > 0, summed, 0.2 * summed).astype(BF16)


def gathered(volume_in, filters_a, bias_a, filters_b, bias_b):
    slices = volume_in.shape[1]
    outputs = filters_a.shape[1]
    extended = jnp.concatenate([shifted(volume_in[:, -1:], "spatial", 1), volume_in], 1)
    full = lax.all_gather(extended, "filter", axis=0, tiled=True)
    hidden = activate(local_conv(full, filters_a, 1, ROWS, COLS), bias_a)
    hidden = hidden.reshape(outputs, slices // 2, ROWS // 2 * (COLS // 2))
    extended = jnp.concatenate([shifted(hidden[:, -1:], "spatial", 1), hidden], 1)
    full = lax.all_gather(extended, "filter", axis=0, tiled=True)
    out = activate(local_conv(full, filters_b, 1, ROWS // 2, COLS // 2), bias_b)
    return out.reshape(filters_b.shape[1], slices // 4, ROWS // 4 * (COLS // 4))


HALF = 2048
QUARTER = 512


def pick_first():
    s = np.zeros((256, 3, 128), np.float32)
    for l in range(3):
        for row in range(2):
            for w in range(64):
                source = 2 * w + l - 1
                if source >= 0:
                    s[row * 128 + source, l, row * 64 + w] = 1
    return s.reshape(256, 384)


def pick_second():
    s = np.zeros((2, 512, 3, 128), np.float32)
    for half in range(2):
        for l in range(3):
            for row in range(4):
                for w in range(32):
                    source = 2 * w + l - 1
                    if source >= 0:
                        s[half, row * 128 + half * 64 + source, l, row * 32 + w] = 1
    return s.reshape(2, 512, 384)


def column(row_of):
    row = lax.broadcasted_iota(jnp.int32, (64, 64), 0)
    col = lax.broadcasted_iota(jnp.int32, (64, 64), 1)
    spread = jnp.broadcast_to(row_of.astype(F32), (64, 64))
    diagonal = jnp.where(row == col, spread, 0.0).astype(BF16)
    return jnp.dot(diagonal, jnp.ones((64, 512), BF16), preferred_element_type=F32)


def leaky(u):
    return jnp.where(u > 0, u, 0.2 * u).astype(BF16)


TAPS_B = tuple(range(9)) + tuple(range(18, 27)) + tuple(range(9, 18))


def kernel(
    n_spatial, xin, fa_in, fb_in, ba_in, bb_in, s1_in, s2_in, out,
    fa, biases, fb, s1, s2, xv, x, xh, wa_send, wa, wb_send, wb, v0, v1, part, sib, y_send, y_recv, hid, v2,
    part2, sib2, z_send, z_recv,
    in_sems, x_sems, sent, halo_sems, wa_sems, wb_sems, sib_sems, y_sems, hid_sems, z_sems,
):
    scope = jax.named_scope
    s = lax.axis_index("spatial")
    f = lax.axis_index("filter")
    core, chip = f % 2, f // 2
    sibling = chip * 2 + (1 - core)
    partner = (1 - chip) * 2 + core
    diagonal = (1 - chip) * 2 + (1 - core)
    slot = core * 2 + chip
    peers = (diagonal, partner, sibling)
    is_first, is_last = s == 0, s == n_spatial - 1
    is_even = s % 2 == 0
    level = (s // 2) % 4
    half = level % 2
    is_odd = s % 2 == 1
    passes_down = level > 0
    even_up = jnp.logical_and(is_even, level == 2)
    odd_up = jnp.logical_and(is_odd, level == 2)
    from_corner = jnp.logical_and(is_odd, level == 3)

    halo_sent = wa_sent = wb_sent = sib_sent = y_sent = hid_sent = sib2_sent = z_sent = sent
    for k in range(3):
        taps = pl.ds(9 * k, 9)
        pltpu.make_async_copy(fa_in.at[taps], fa.at[taps], in_sems.at[3]).start()
    load_fa = pltpu.make_async_copy(fa_in, fa, in_sems.at[3])

    def x_load(c):
        lanes = pl.ds(pl.multiple_of(c * 2048, 2048), 2048)
        return pltpu.make_async_copy(xin.at[:, :, lanes], xv.at[:, :, lanes], x_sems.at[c])

    for c in range(4):
        x_load(c).start()
    load_s1 = pltpu.make_async_copy(s1_in, s1, in_sems.at[1])
    load_fb = pltpu.make_async_copy(fb_in, fb, in_sems.at[0])
    load_ba = pltpu.make_async_copy(ba_in, biases.at[0], in_sems.at[4])
    load_bb = pltpu.make_async_copy(bb_in, biases.at[1], in_sems.at[4])
    load_s2 = pltpu.make_async_copy(s2_in, s2, in_sems.at[2])
    load_s1.start()
    load_fb.start()
    load_ba.start()
    load_bb.start()
    load_s2.start()
    barrier = pltpu.get_barrier_semaphore()
    for peer in peers:
        pl.semaphore_signal(barrier, inc=1, device_id=(s, peer), device_id_type=MESH)
    for step in (1, 2):

        @pl.when(s < n_spatial - step)
        def _():
            pl.semaphore_signal(barrier, inc=1, device_id=(s + step, f), device_id_type=MESH)

        @pl.when(s >= step)
        def _():
            pl.semaphore_signal(barrier, inc=1, device_id=(s - step, f), device_id_type=MESH)

    @pl.when(from_corner)
    def _():
        pl.semaphore_signal(barrier, inc=1, device_id=(s - 3, f), device_id_type=MESH)

    def pack_a(g):
        to = (g % 2) * 2 + g // 2
        for b in range(7):
            parts = [fa[t][:, 32 * g : 32 * g + 32] for t in range(4 * b, min(4 * b + 4, 27))]
            if len(parts) < 4:
                parts.append(jnp.zeros((64, 32), BF16))
            block = jnp.concatenate(parts, axis=1)
            for q in range(2):
                wa_send[to, q, :, 128 * b : 128 * b + 128] = block[32 * q : 32 * q + 32]

    def pack_blocks(of_chip):
        for k in range(2):

            @pl.when(of_chip == k)
            def _():
                pack_a(2 * k)
                pack_a(2 * k + 1)

    with scope("load_fa"):
        load_fa.wait()
    with scope("pack_a"):
        pack_blocks(1 - chip)

    with scope("barrier"):
        neighbours = jnp.minimum(s, 2) + jnp.minimum(n_spatial - 1 - s, 2)
        pl.semaphore_wait(barrier, 3 + neighbours + jnp.where(even_up, 1, 0))

    def remote(src, dst, sent, here, target):
        return pltpu.make_async_remote_copy(
            src_ref=src, dst_ref=dst, send_sem=sent, recv_sem=here,
            device_id=target, device_id_type=MESH,
        )

    def slot_of(peer):
        return (peer % 2) * 2 + peer // 2

    near = (s, sibling)

    def to_sibling(send, dst, sent, here):
        return remote(send.at[slot_of(sibling)], dst.at[slot], sent, here, near)

    def own_half(m):
        return remote(
            wb_send.at[slot_of(peers[m]), half], wb.at[slot, half], wb_sent, wb_sems.at[m],
            (s, peers[m]),
        )

    def pass_on(m):
        block = wb.at[slot_of(peers[m]), half]

        def to(step):
            remote(block, block, wb_sent, wb_sems.at[2], (s + step, f)).start()

        @pl.when(passes_down)
        def _():
            to(-2)

        @pl.when(even_up)
        def _():
            to(2)

        @pl.when(even_up if m == 1 else odd_up)
        def _():
            to(3 if m == 1 else 2)

    def slots(send, dst, sent, here, n):
        return remote(send.at[pl.ds(0, n)], dst.at[pl.ds(0, n)], sent, here, near)

    wa_half = remote(
        wa_send.at[slot_of(partner), half], wa.at[slot, half], wa_sent, wa_sems.at[0], (s, partner)
    )

    def wa_whole(peer):
        return remote(wa_send.at[slot_of(peer)], wa.at[slot], wa_sent, wa_sems.at[1], (s, peer))

    @pl.when(core == 1)
    def _():
        wa_half.start()
        wa_whole(diagonal).start()

    @pl.when(core == 0)
    def _():
        wa_whole(partner).start()

    with scope("pack_a"):
        pack_blocks(chip)
    wa_whole(sibling).start()

    def pass_wa():
        wa_half.wait_recv()
        block = wa.at[slot_of(partner), half]

        def to(step):
            remote(block, block, wa_sent, wa_sems.at[2], (s + step, f)).start()

        @pl.when(passes_down)
        def _():
            to(-2)

        @pl.when(even_up)
        def _():
            to(2)
            to(3)

    wa[slot] = wa_send[slot]

    def halo_copy(c):
        lanes = pl.ds(pl.multiple_of(c * 2048, 2048), 2048)
        return remote(
            x.at[pl.ds(96, 32), lanes], xh.at[:, lanes], halo_sent, halo_sems.at[jnp.maximum(c - 1, 0)], (s + 1, f)
        )

    def by_slice(q):
        lanes = pl.ds(pl.multiple_of(q * 512, 512), 512)
        rows = jnp.swapaxes(xv[:, :, lanes], 0, 1)
        for k in range(4):
            x[32 * k : 32 * k + 32, lanes] = rows[k]

    with scope("slices"):

        def body(c, carry):
            x_load(c).wait()
            for q in range(4):
                by_slice(4 * c + q)

            @pl.when(jnp.logical_not(is_last))
            def _():
                halo_copy(c).start()

            return carry

        lax.fori_loop(0, 4, body, 0)

    @pl.when(core == 0)
    def _():
        wa_whole(diagonal).start()

    with scope("pack_b"):
        load_fb.wait()
        for g in range(4):
            to = (g % 2) * 2 + g // 2
            for b in range(14):
                parts = [fb[t][:, 64 * g : 64 * g + 64] for t in TAPS_B[2 * b : 2 * b + 2]]
                if len(parts) < 2:
                    parts.append(jnp.zeros((64, 64), BF16))
                block = jnp.concatenate(parts, axis=1)
                for q in range(2):
                    wb_send[to, q, :, 128 * b : 128 * b + 128] = block[32 * q : 32 * q + 32]
        wb[slot] = wb_send[slot]

    def rows_of(ref, t):
        def row(r):
            return ref[:, pl.ds(pl.multiple_of(r * 128, 128), 128)]

        before = jnp.where(t > 0, row(jnp.maximum(4 * t - 1, 0)), jnp.zeros((), BF16))
        one = row(4 * t + 1)
        return (
            jnp.concatenate([before, one], 1),
            jnp.concatenate([row(4 * t), row(4 * t + 2)], 1),
            jnp.concatenate([one, row(4 * t + 3)], 1),
        )

    def taps_own(t, carry):
        cells = jnp.concatenate(rows_of(x, t), 0)
        picked = jnp.dot(cells, s1[...], preferred_element_type=F32).astype(BF16)
        lanes = pl.ds(pl.multiple_of(t * 128, 128), 128)
        for j in range(3):
            for l in range(3):
                for k in range(4):
                    piece = picked[j * 128 + k * 32 : j * 128 + k * 32 + 32, l * 128 : l * 128 + 128]
                    if k > 0:
                        at = ((k - 1) * 9 + 3 * j + l) * 32
                        v1[at : at + 32, lanes] = piece
                    if k < 2:
                        at = ((k + 1) * 9 + 3 * j + l) * 32
                        v0[at : at + 32, lanes] = piece
        return carry

    v0[864:896] = jnp.zeros((32, HALF), BF16)
    v1[864:896] = jnp.zeros((32, HALF), BF16)
    load_s1.wait()
    with scope("taps"):
        lax.fori_loop(0, 16, taps_own, 0, unroll=4)
    with scope("pass_wa"):
        pl.when(core == 1)(pass_wa)
    own_half(0).start()

    def taps_halo(q):
        cells = jnp.concatenate([c for t in range(4) for c in rows_of(xh, 4 * q + t)], 0)
        picked = jnp.dot(cells, s1[...], preferred_element_type=F32).astype(BF16)
        for t in range(4):
            lanes = pl.ds(pl.multiple_of((4 * q + t) * 128, 128), 128)
            for j in range(3):
                for l in range(3):
                    at = (3 * j + l) * 32
                    row = (3 * t + j) * 32
                    v0[at : at + 32, lanes] = picked[row : row + 32, l * 128 : l * 128 + 128]

    def sib_copy(h, c):
        return remote(part.at[h, c, 1 - core], sib.at[h, c], sib_sent, sib_sems.at[h, c], near)

    def y_copy(h, c):
        return remote(y_send.at[h, c], y_recv.at[h, c], y_sent, y_sems.at[h, c], (s, partner))

    def across(h, c):
        sib_copy(h, c).wait_recv()
        y_send[h, c] = (part[h, c, core, 1 - chip] + sib[h, c, 1 - chip]).astype(BF16)
        y_copy(h, c).start()

    def first_conv(h, v, c):
        lanes = pl.ds(pl.multiple_of(c * 512, 512), 512)
        sums = jnp.dot(wa[...].reshape(256, 896), v[:, lanes], preferred_element_type=F32)
        part[h, c] = sums.reshape(2, 2, 64, 512)
        sib_copy(h, c).start()

    def hid_copy(c):
        return remote(hid.at[2, c], hid.at[0, c], hid_sent, hid_sems.at[max(c - 1, 0)], (s + 1, f))

    hid_all = remote(hid.at[2], hid.at[0], hid_sent, hid_sems.at[0], near)
    load_ba.wait()
    load_bb.wait()
    bias_a = column(biases[0])

    def finish(h, slot_h, c):
        y_copy(h, c).wait_recv()
        total = part[h, c, core, chip] + sib[h, c, chip] + y_recv[h, c].astype(F32) + bias_a
        hid[slot_h, c] = leaky(total)
        if slot_h == 2:

            @pl.when(jnp.logical_not(is_last))
            def _():
                hid_copy(c).start()

    def second_taps(i, at_i, quarters):
        def block(q):
            return hid[i, q // 4, :, 128 * (q % 4) : 128 * (q % 4) + 128]

        zero = jnp.zeros((64, 128), BF16)
        now = jnp.concatenate(
            [jnp.concatenate([block(4 * u + r) for r in range(4)], 1) for u in quarters], 0
        )
        before = jnp.concatenate(
            [
                jnp.concatenate([block(4 * u + r - 1) if 4 * u + r else zero for r in range(4)], 1)
                for u in quarters
            ],
            0,
        )
        for j, (cells, half) in enumerate(((before, 1), (now, 0), (now, 1))):
            picked = jnp.dot(cells, s2[half], preferred_element_type=F32).astype(BF16)
            for n, u in enumerate(quarters):
                for l in range(3):
                    at = (at_i * 9 + 3 * j + l) * 64
                    v2[at : at + 64, 128 * u : 128 * u + 128] = picked[
                        64 * n : 64 * n + 64, 128 * l : 128 * l + 128
                    ]

    with scope("wait_wa"):

        @pl.when(core == 0)
        def _():
            slots(wa_send, wa, wa_sent, wa_sems.at[1], 3).wait_recv()

        @pl.when(core == 1)
        def _():
            slots(wa_send, wa, wa_sent, wa_sems.at[1], 2).wait_recv()
            remote(wa_send.at[0, 0], wa.at[0, 0], wa_sent, wa_sems.at[2], near).wait_recv()
    pl.when(core == 0)(own_half(1).start)

    with scope("conv_d1"):

        def conv_d1(c, carry):
            first_conv(1, v1, c)
            return carry

        def conv_and_send(c, carry):
            first_conv(1, v1, c)
            across(1, c)
            return carry

        def send_one(c, carry):
            across(1, c)
            return carry

        @pl.when(core == 0)
        def _():
            lax.fori_loop(0, 4, conv_d1, 0)
            lax.fori_loop(0, 3, send_one, 0)

        @pl.when(core == 1)
        def _():
            conv_and_send(0, 0)
            own_half(1).start()
            lax.fori_loop(1, 3, conv_and_send, 0)
            conv_d1(3, 0)

    @pl.when(is_first)
    def _():
        xh[...] = jnp.zeros(xh.shape, BF16)
        hid[0] = jnp.zeros((4, 64, 512), BF16)

    def conv_d0(c):
        with scope("halo_wait"):

            @pl.when(jnp.logical_not(is_first))
            def _():
                if c == 0:
                    lanes = pl.ds(0, 4096)
                    block = xh.at[:, lanes]
                    remote(block, block, halo_sent, halo_sems.at[0], near).wait_recv()
                elif c > 1:
                    halo_copy(c).wait_recv()

        with scope("conv_d0"):
            taps_halo(c)
            first_conv(0, v0, c)

    def finish_d1(c):
        with scope("finish_d1"):
            finish(1, 2, c)

    def send_sums(h, c):
        with scope("across"):
            across(h, c)

    def finish_d0(c):
        with scope("finish_d0"):
            finish(0, 1, c)

    def pass_wb(m):
        with scope("pass_wb"):
            own_half(m).wait_recv()
            pass_on(m)

    def taps2(i, at_i, quarters):
        with scope("taps2"):
            second_taps(i, at_i, quarters)

    to_sibling(wb_send, wb, wb_sent, wb_sems.at[2]).start()
    conv_d0(0)
    conv_d0(1)
    pass_wb(0)
    conv_d0(2)
    pass_wb(1)
    finish_d1(0)
    send_sums(1, 3)
    finish_d1(1)
    send_sums(0, 0)
    conv_d0(3)
    finish_d1(2)
    send_sums(0, 1)
    finish_d1(3)
    send_sums(0, 2)
    load_s2.wait()
    v2[1728:1792] = jnp.zeros((64, QUARTER), BF16)
    taps2(2, 1, range(4))
    finish_d0(0)
    send_sums(0, 3)

    def halo_taps(quarters):
        with scope("hid_wait"):

            @pl.when(jnp.logical_not(is_first))
            def _():
                if len(quarters) == 2:
                    block = hid.at[0, pl.ds(0, 2)]
                    remote(block, block, hid_sent, hid_sems.at[0], near).wait_recv()
                else:
                    hid_copy(quarters[0]).wait_recv()

        taps2(0, 0, quarters)

    halo_taps((0, 1))
    finish_d0(1)
    taps2(1, 2, (0, 1))
    with scope("wait_wb"):
        slots(wb_send, wb, wb_sent, wb_sems.at[2], 2).wait_recv()

    units = ((0, 1), (2,), (3,))

    def unit_lanes(n):
        return pl.ds(128 * units[n][0], 128 * len(units[n]))

    def sib2_copy(n):
        lanes = unit_lanes(n)
        return remote(
            part2.at[1 - core, chip, :, lanes], sib2.at[:, lanes], sib2_sent, z_sems.at[n], near
        )

    def z_copy(n, k):
        lanes = unit_lanes(n)
        return remote(
            z_send.at[k, :, lanes], z_recv.at[core, :, lanes], z_sent, z_sems.at[n],
            (s, (1 - chip) * 2 + k),
        )

    def conv2(n, rows, at):
        lanes = unit_lanes(n)
        sums = jnp.dot(
            wb[:, :, :, at : at + rows].reshape(256, rows),
            v2[at : at + rows, lanes],
            preferred_element_type=F32,
        )
        return sums.reshape(2, 2, 64, 128 * len(units[n]))

    for n, quarters in enumerate(units):
        lanes = unit_lanes(n)
        if n > 0:
            halo_taps((n + 1,))
            if n == 2:
                with scope("conv2_sides"):
                    part2[:, :, :, lanes] = conv2(n, 1152, 0)
            finish_d0(n + 1)
            taps2(1, 2, (n + 1,))
        with scope("conv2"):
            if n == 2:
                part2[:, :, :, lanes] = part2[:, :, :, lanes] + conv2(n, 640, 1152)
            else:
                part2[:, :, :, lanes] = conv2(n, 1792, 0)
            for k in range(2):
                z_send[k, :, lanes] = part2[k, 1 - chip, :, lanes].astype(BF16)
                z_copy(n, k).start()
            sib2_copy(n).start()
    bias_b = column(biases[1])
    for n, quarters in enumerate(units):
        lanes = unit_lanes(n)
        with scope("z_wait"):
            arrived = part2.at[0, :, :, lanes]
            remote(arrived, arrived, z_sent, z_sems.at[n], near).wait_recv()
        far = z_recv[0, :, lanes].astype(F32) + z_recv[1, :, lanes].astype(F32)
        bias = bias_b[:, : 128 * len(quarters)]
        total = part2[core, chip, :, lanes] + sib2[:, lanes] + far + bias
        out[:, lanes] = leaky(total)

    with scope("drain"):
        slots(wa_send, wa, wa_sent, wa_sems.at[1], 2).wait_send()

        @pl.when(core == 0)
        def _():
            slots(wa_send, wa, wa_sent, wa_sems.at[1], 1).wait_send()

        @pl.when(core == 1)
        def _():
            wa_half.wait_send()

        @pl.when(jnp.logical_and(core == 1, passes_down))
        def _():
            wa_half.wait_send()

        @pl.when(jnp.logical_and(core == 1, even_up))
        def _():
            slots(wa_send, wa, wa_sent, wa_sems.at[1], 1).wait_send()

        slots(wb_send, wb, wb_sent, wb_sems.at[2], 2).wait_send()

        @pl.when(passes_down)
        def _():
            slots(wb_send, wb, wb_sent, wb_sems.at[2], 1).wait_send()

        @pl.when(even_up)
        def _():
            slots(wb_send, wb, wb_sent, wb_sems.at[2], 1).wait_send()

        @pl.when(level == 2)
        def _():
            own_half(0).wait_send()

        remote(part.at[:, :, 1 - core], sib, sib_sent, sib_sems.at[0, 0], near).wait_send()
        remote(y_send, y_recv, y_sent, y_sems.at[0, 0], near).wait_send()
        remote(part2.at[1 - core, chip], sib2, sib2_sent, z_sems.at[0], near).wait_send()
        remote(z_send, z_recv, z_sent, z_sems.at[0], near).wait_send()

        @pl.when(jnp.logical_not(is_last))
        def _():
            remote(x.at[pl.ds(96, 32)], xh, halo_sent, halo_sems.at[0], near).wait_send()
            hid_all.wait_send()


def scattered(n_spatial, volume_in, filters_a, bias_a, filters_b, bias_b):
    vmem = pl.BlockSpec(memory_space=pltpu.VMEM)
    hbm = pl.BlockSpec(memory_space=pltpu.HBM)
    dma = pltpu.SemaphoreType.DMA

    def body(*refs):
        kernel(n_spatial, *refs)

    out = pl.pallas_call(
        body,
        out_shape=jax.ShapeDtypeStruct((64, QUARTER), BF16),
        in_specs=[hbm] * 7,
        out_specs=vmem,
        scratch_shapes=[
            pltpu.VMEM((27, 64, 128), BF16),
            pltpu.VMEM((2, 1, 64), BF16),
            pltpu.VMEM((27, 64, 256), BF16),
            pltpu.VMEM((256, 384), BF16),
            pltpu.VMEM((2, 512, 384), BF16),
            pltpu.VMEM((32, 4, ROWS * COLS), BF16),
            pltpu.VMEM((128, ROWS * COLS), BF16),
            pltpu.VMEM((32, ROWS * COLS), BF16),
            pltpu.VMEM((4, 2, 32, 896), BF16),
            pltpu.VMEM((4, 2, 32, 896), BF16),
            pltpu.VMEM((4, 2, 32, 1792), BF16),
            pltpu.VMEM((4, 2, 32, 1792), BF16),
            pltpu.VMEM((896, HALF), BF16),
            pltpu.VMEM((896, HALF), BF16),
            pltpu.VMEM((2, 4, 2, 2, 64, 512), F32),
            pltpu.VMEM((2, 4, 2, 64, 512), F32),
            pltpu.VMEM((2, 4, 64, 512), BF16),
            pltpu.VMEM((2, 4, 64, 512), BF16),
            pltpu.VMEM((3, 4, 64, 512), BF16),
            pltpu.VMEM((1792, QUARTER), BF16),
            pltpu.VMEM((2, 2, 64, 512), F32),
            pltpu.VMEM((64, 512), F32),
            pltpu.VMEM((2, 64, 512), BF16),
            pltpu.VMEM((2, 64, 512), BF16),
            dma((5,)), dma((4,)), dma, dma((3,)), dma((3,)), dma((3,)), dma((2, 4)), dma((2, 4)), dma((3,)),
            dma((3,)),
        ],
        compiler_params=pltpu.CompilerParams(
            collective_id=0, has_side_effects=True, vmem_limit_bytes=52 * 1024 * 1024
        ),
        name="scattered_convs",
    )(
        *(
            pltpu.with_memory_space_constraint(a, pltpu.HBM)
            for a in (
                volume_in,
                filters_a,
                filters_b,
                bias_a.reshape(1, 64),
                bias_b.reshape(1, 64),
                jnp.asarray(pick_first(), BF16),
                jnp.asarray(pick_second(), BF16),
            )
        )
    )
    return out.reshape(64, 1, QUARTER)


def per_device(volume_in, filters_a, bias_a, filters_b, bias_b):
    n_spatial = lax.axis_size("spatial")
    own = volume_in.shape == (32, 4, ROWS * COLS) and filters_b.shape == (27, 64, 256)
    if own and n_spatial % 8 == 0:
        return scattered(n_spatial, volume_in, filters_a, bias_a, filters_b, bias_b)
    return gathered(volume_in, filters_a, bias_a, filters_b, bias_b)


def solution(mesh):
    in_specs = (
        P("filter", "spatial", None),
        P(None, "filter", None),
        P("filter"),
        P(None, "filter", None),
        P("filter"),
    )
    return jax.shard_map(
        per_device,
        mesh=mesh,
        in_specs=in_specs,
        out_specs=P("filter", "spatial", None),
        check_vma=False,
    )
```

```python
import jax
import jax.numpy as jnp
import numpy as np
from jax import lax
from jax.experimental import pallas as pl
from jax.experimental.pallas import tpu as pltpu
from jax.sharding import PartitionSpec as P

MESH = pl.DeviceIdType.MESH
ROWS = 64
COLS = 128
F32 = jnp.float32
BF16 = jnp.bfloat16


def shifted(block, axis, distance):
    devices = range(lax.axis_size(axis))
    route = [(i - distance, i) for i in devices if i - distance in devices]
    return lax.ppermute(block, axis, route)


def local_conv(block, weight, pad_rows, row_count, col_count):
    channels = block.shape[0]
    slices = block.shape[1]
    volume = block.reshape(1, channels, slices, row_count, col_count)
    kernel = weight.reshape(3, 3, 3, weight.shape[1], weight.shape[2])
    return lax.conv_general_dilated(
        volume,
        kernel,
        (2, 2, 2),
        ((0, 0), (pad_rows, pad_rows), (1, 1)),
        dimension_numbers=("NCDHW", "DHWOI", "NCDHW"),
        preferred_element_type=F32,
    )[0]


def activate(summed, bias_vec):
    summed = summed + bias_vec.astype(F32)[:, None, None, None]
    return jnp.where(summed > 0, summed, 0.2 * summed).astype(BF16)


def gathered(volume_in, filters_a, bias_a, filters_b, bias_b):
    slices = volume_in.shape[1]
    outputs = filters_a.shape[1]
    extended = jnp.concatenate([shifted(volume_in[:, -1:], "spatial", 1), volume_in], 1)
    full = lax.all_gather(extended, "filter", axis=0, tiled=True)
    hidden = activate(local_conv(full, filters_a, 1, ROWS, COLS), bias_a)
    hidden = hidden.reshape(outputs, slices // 2, ROWS // 2 * (COLS // 2))
    extended = jnp.concatenate([shifted(hidden[:, -1:], "spatial", 1), hidden], 1)
    full = lax.all_gather(extended, "filter", axis=0, tiled=True)
    out = activate(local_conv(full, filters_b, 1, ROWS // 2, COLS // 2), bias_b)
    return out.reshape(filters_b.shape[1], slices // 4, ROWS // 4 * (COLS // 4))


HALF = 2048
QUARTER = 512


def pick_first():
    s = np.zeros((256, 3, 128), np.float32)
    for l in range(3):
        for row in range(2):
            for w in range(64):
                source = 2 * w + l - 1
                if source >= 0:
                    s[row * 128 + source, l, row * 64 + w] = 1
    return s.reshape(256, 384)


def pick_second():
    s = np.zeros((2, 512, 3, 128), np.float32)
    for half in range(2):
        for l in range(3):
            for row in range(4):
                for w in range(32):
                    source = 2 * w + l - 1
                    if source >= 0:
                        s[half, row * 128 + half * 64 + source, l, row * 32 + w] = 1
    return s.reshape(2, 512, 384)


def column(row_of):
    row = lax.broadcasted_iota(jnp.int32, (64, 64), 0)
    col = lax.broadcasted_iota(jnp.int32, (64, 64), 1)
    spread = jnp.broadcast_to(row_of.astype(F32), (64, 64))
    diagonal = jnp.where(row == col, spread, 0.0).astype(BF16)
    return jnp.dot(diagonal, jnp.ones((64, 512), BF16), preferred_element_type=F32)


def leaky(u):
    return jnp.where(u > 0, u, 0.2 * u).astype(BF16)


TAPS_B = tuple(range(9)) + tuple(range(18, 27)) + tuple(range(9, 18))


def kernel(
    n_spatial, xin, fa_in, fb_in, ba_in, bb_in, s1_in, s2_in, out,
    fa, biases, fb, s1, s2, xv, x, xh, wa_send, wa, wb_send, wb, v0, v1, part, sib, y_send, y_recv, hid, v2,
    part2, sib2, z_send, z_recv,
    in_sems, x_sems, sent, halo_sems, wa_sems, wb_sems, sib_sems, y_sems, hid_sems, z_sems,
):
    scope = jax.named_scope
    s = lax.axis_index("spatial")
    f = lax.axis_index("filter")
    core, chip = f % 2, f // 2
    sibling = chip * 2 + (1 - core)
    partner = (1 - chip) * 2 + core
    diagonal = (1 - chip) * 2 + (1 - core)
    slot = core * 2 + chip
    peers = (diagonal, partner, sibling)
    is_first, is_last = s == 0, s == n_spatial - 1
    is_even = s % 2 == 0
    level = (s // 2) % 4
    half = level % 2
    is_odd = s % 2 == 1
    passes_down = level > 0
    even_up = jnp.logical_and(is_even, level == 2)
    odd_up = jnp.logical_and(is_odd, level == 2)
    from_corner = jnp.logical_and(is_odd, level == 3)

    halo_sent = wa_sent = wb_sent = sib_sent = y_sent = hid_sent = sib2_sent = z_sent = sent
    for k in range(3):
        taps = pl.ds(9 * k, 9)
        pltpu.make_async_copy(fa_in.at[taps], fa.at[taps], in_sems.at[3]).start()
    load_fa = pltpu.make_async_copy(fa_in, fa, in_sems.at[3])

    def x_load(c):
        lanes = pl.ds(pl.multiple_of(c * 2048, 2048), 2048)
        return pltpu.make_async_copy(xin.at[:, :, lanes], xv.at[:, :, lanes], x_sems.at[c])

    for c in range(4):
        x_load(c).start()
    load_s1 = pltpu.make_async_copy(s1_in, s1, in_sems.at[1])
    load_fb = pltpu.make_async_copy(fb_in, fb, in_sems.at[0])
    load_ba = pltpu.make_async_copy(ba_in, biases.at[0], in_sems.at[4])
    load_bb = pltpu.make_async_copy(bb_in, biases.at[1], in_sems.at[4])
    load_s2 = pltpu.make_async_copy(s2_in, s2, in_sems.at[2])
    load_s1.start()
    load_fb.start()
    load_ba.start()
    load_bb.start()
    load_s2.start()
    barrier = pltpu.get_barrier_semaphore()
    for peer in peers:
        pl.semaphore_signal(barrier, inc=1, device_id=(s, peer), device_id_type=MESH)
    for step in (1, 2):

        @pl.when(s < n_spatial - step)
        def _():
            pl.semaphore_signal(barrier, inc=1, device_id=(s + step, f), device_id_type=MESH)

        @pl.when(s >= step)
        def _():
            pl.semaphore_signal(barrier, inc=1, device_id=(s - step, f), device_id_type=MESH)

    @pl.when(from_corner)
    def _():
        pl.semaphore_signal(barrier, inc=1, device_id=(s - 3, f), device_id_type=MESH)

    def pack_a(g):
        to = (g % 2) * 2 + g // 2
        for b in range(7):
            parts = [fa[t][:, 32 * g : 32 * g + 32] for t in range(4 * b, min(4 * b + 4, 27))]
            if len(parts) < 4:
                parts.append(jnp.zeros((64, 32), BF16))
            block = jnp.concatenate(parts, axis=1)
            for q in range(2):
                wa_send[to, q, :, 128 * b : 128 * b + 128] = block[32 * q : 32 * q + 32]

    def pack_blocks(of_chip):
        for k in range(2):

            @pl.when(of_chip == k)
            def _():
                pack_a(2 * k)
                pack_a(2 * k + 1)

    with scope("load_fa"):
        load_fa.wait()
    with scope("pack_a"):
        pack_blocks(1 - chip)

    with scope("barrier"):
        neighbours = jnp.minimum(s, 2) + jnp.minimum(n_spatial - 1 - s, 2)
        pl.semaphore_wait(barrier, 3 + neighbours + jnp.where(even_up, 1, 0))

    def remote(src, dst, sent, here, target):
        return pltpu.make_async_remote_copy(
            src_ref=src, dst_ref=dst, send_sem=sent, recv_sem=here,
            device_id=target, device_id_type=MESH,
        )

    def slot_of(peer):
        return (peer % 2) * 2 + peer // 2

    near = (s, sibling)

    def to_sibling(send, dst, sent, here):
        return remote(send.at[slot_of(sibling)], dst.at[slot], sent, here, near)

    def own_half(m):
        return remote(
            wb_send.at[slot_of(peers[m]), half], wb.at[slot, half], wb_sent, wb_sems.at[m],
            (s, peers[m]),
        )

    def pass_on(m):
        block = wb.at[slot_of(peers[m]), half]

        def to(step):
            remote(block, block, wb_sent, wb_sems.at[2], (s + step, f)).start()

        @pl.when(passes_down)
        def _():
            to(-2)

        @pl.when(even_up)
        def _():
            to(2)

        @pl.when(even_up if m == 1 else odd_up)
        def _():
            to(3 if m == 1 else 2)

    def slots(send, dst, sent, here, n):
        return remote(send.at[pl.ds(0, n)], dst.at[pl.ds(0, n)], sent, here, near)

    wa_half = remote(
        wa_send.at[slot_of(partner), half], wa.at[slot, half], wa_sent, wa_sems.at[0], (s, partner)
    )

    def wa_whole(peer):
        return remote(wa_send.at[slot_of(peer)], wa.at[slot], wa_sent, wa_sems.at[1], (s, peer))

    @pl.when(core == 1)
    def _():
        wa_half.start()
        wa_whole(diagonal).start()

    @pl.when(core == 0)
    def _():
        wa_whole(partner).start()

    with scope("pack_a"):
        pack_blocks(chip)
    wa_whole(sibling).start()

    def pass_wa():
        wa_half.wait_recv()
        block = wa.at[slot_of(partner), half]

        def to(step):
            remote(block, block, wa_sent, wa_sems.at[2], (s + step, f)).start()

        @pl.when(passes_down)
        def _():
            to(-2)

        @pl.when(even_up)
        def _():
            to(2)
            to(3)

    wa[slot] = wa_send[slot]

    def halo_copy(c):
        lanes = pl.ds(pl.multiple_of(c * 2048, 2048), 2048)
        return remote(
            x.at[pl.ds(96, 32), lanes], xh.at[:, lanes], halo_sent, halo_sems.at[jnp.maximum(c - 1, 0)], (s + 1, f)
        )

    def by_slice(q):
        lanes = pl.ds(pl.multiple_of(q * 512, 512), 512)
        rows = jnp.swapaxes(xv[:, :, lanes], 0, 1)
        for k in range(4):
            x[32 * k : 32 * k + 32, lanes] = rows[k]

    with scope("slices"):

        def body(c, carry):
            x_load(c).wait()
            for q in range(4):
                by_slice(4 * c + q)

            @pl.when(jnp.logical_not(is_last))
            def _():
                halo_copy(c).start()

            return carry

        lax.fori_loop(0, 4, body, 0)

    @pl.when(core == 0)
    def _():
        wa_whole(diagonal).start()

    with scope("pack_b"):
        load_fb.wait()
        for g in range(4):
            to = (g % 2) * 2 + g // 2
            for b in range(14):
                parts = [fb[t][:, 64 * g : 64 * g + 64] for t in TAPS_B[2 * b : 2 * b + 2]]
                if len(parts) < 2:
                    parts.append(jnp.zeros((64, 64), BF16))
                block = jnp.concatenate(parts, axis=1)
                for q in range(2):
                    wb_send[to, q, :, 128 * b : 128 * b + 128] = block[32 * q : 32 * q + 32]
        wb[slot] = wb_send[slot]

    def rows_of(ref, t):
        def row(r):
            return ref[:, pl.ds(pl.multiple_of(r * 128, 128), 128)]

        before = jnp.where(t > 0, row(jnp.maximum(4 * t - 1, 0)), jnp.zeros((), BF16))
        one = row(4 * t + 1)
        return (
            jnp.concatenate([before, one], 1),
            jnp.concatenate([row(4 * t), row(4 * t + 2)], 1),
            jnp.concatenate([one, row(4 * t + 3)], 1),
        )

    def taps_own(t, carry):
        cells = jnp.concatenate(rows_of(x, t), 0)
        picked = jnp.dot(cells, s1[...], preferred_element_type=F32).astype(BF16)
        lanes = pl.ds(pl.multiple_of(t * 128, 128), 128)
        for j in range(3):
            for l in range(3):
                for k in range(4):
                    piece = picked[j * 128 + k * 32 : j * 128 + k * 32 + 32, l * 128 : l * 128 + 128]
                    if k > 0:
                        at = ((k - 1) * 9 + 3 * j + l) * 32
                        v1[at : at + 32, lanes] = piece
                    if k < 2:
                        at = ((k + 1) * 9 + 3 * j + l) * 32
                        v0[at : at + 32, lanes] = piece
        return carry

    v0[864:896] = jnp.zeros((32, HALF), BF16)
    v1[864:896] = jnp.zeros((32, HALF), BF16)
    load_s1.wait()
    with scope("taps"):
        lax.fori_loop(0, 16, taps_own, 0, unroll=4)
    with scope("pass_wa"):
        pl.when(core == 1)(pass_wa)
    own_half(0).start()

    def taps_halo(q):
        cells = jnp.concatenate([c for t in range(4) for c in rows_of(xh, 4 * q + t)], 0)
        picked = jnp.dot(cells, s1[...], preferred_element_type=F32).astype(BF16)
        for t in range(4):
            lanes = pl.ds(pl.multiple_of((4 * q + t) * 128, 128), 128)
            for j in range(3):
                for l in range(3):
                    at = (3 * j + l) * 32
                    row = (3 * t + j) * 32
                    v0[at : at + 32, lanes] = picked[row : row + 32, l * 128 : l * 128 + 128]

    def sib_copy(h, c):
        here = sib_sems.at[c if h == 1 else 4 + c // 3]
        return remote(part.at[h, c, 1 - core], sib.at[h, c], sib_sent, here, near)

    def y_copy(h, c):
        return remote(y_send.at[h, c], y_recv.at[h, c], y_sent, y_sems.at[h, c], (s, partner))

    def across(h, c):
        if h == 1 or c == 3:
            sib_copy(h, c).wait_recv()
        elif c == 0:
            block = sib.at[0, pl.ds(0, 3)]
            remote(block, block, sib_sent, sib_sems.at[4], near).wait_recv()
        y_send[h, c] = (part[h, c, core, 1 - chip] + sib[h, c, 1 - chip]).astype(BF16)
        y_copy(h, c).start()

    def first_conv(h, v, c):
        lanes = pl.ds(pl.multiple_of(c * 512, 512), 512)
        sums = jnp.dot(wa[...].reshape(256, 896), v[:, lanes], preferred_element_type=F32)
        part[h, c] = sums.reshape(2, 2, 64, 512)
        sib_copy(h, c).start()

    def hid_copy(c):
        return remote(hid.at[2, c], hid.at[0, c], hid_sent, hid_sems.at[max(c - 1, 0)], (s + 1, f))

    hid_all = remote(hid.at[2], hid.at[0], hid_sent, hid_sems.at[0], near)
    load_ba.wait()
    load_bb.wait()
    bias_a = column(biases[0])

    def finish(h, slot_h, c):
        y_copy(h, c).wait_recv()
        total = part[h, c, core, chip] + sib[h, c, chip] + y_recv[h, c].astype(F32) + bias_a
        hid[slot_h, c] = leaky(total)
        if slot_h == 2:

            @pl.when(jnp.logical_not(is_last))
            def _():
                hid_copy(c).start()

    def second_taps(i, at_i, quarters):
        def block(q):
            return hid[i, q // 4, :, 128 * (q % 4) : 128 * (q % 4) + 128]

        zero = jnp.zeros((64, 128), BF16)
        now = jnp.concatenate(
            [jnp.concatenate([block(4 * u + r) for r in range(4)], 1) for u in quarters], 0
        )
        before = jnp.concatenate(
            [
                jnp.concatenate([block(4 * u + r - 1) if 4 * u + r else zero for r in range(4)], 1)
                for u in quarters
            ],
            0,
        )
        for j, (cells, half) in enumerate(((before, 1), (now, 0), (now, 1))):
            picked = jnp.dot(cells, s2[half], preferred_element_type=F32).astype(BF16)
            for n, u in enumerate(quarters):
                for l in range(3):
                    at = (at_i * 9 + 3 * j + l) * 64
                    v2[at : at + 64, 128 * u : 128 * u + 128] = picked[
                        64 * n : 64 * n + 64, 128 * l : 128 * l + 128
                    ]

    with scope("wait_wa"):

        @pl.when(core == 0)
        def _():
            slots(wa_send, wa, wa_sent, wa_sems.at[1], 3).wait_recv()

        @pl.when(core == 1)
        def _():
            slots(wa_send, wa, wa_sent, wa_sems.at[1], 2).wait_recv()
            remote(wa_send.at[0, 0], wa.at[0, 0], wa_sent, wa_sems.at[2], near).wait_recv()
    pl.when(core == 0)(own_half(1).start)

    with scope("conv_d1"):

        def conv_d1(c, carry):
            first_conv(1, v1, c)
            return carry

        def conv_and_send(c, carry):
            first_conv(1, v1, c)
            across(1, c)
            return carry

        def send_one(c, carry):
            across(1, c)
            return carry

        @pl.when(core == 0)
        def _():
            lax.fori_loop(0, 4, conv_d1, 0)
            lax.fori_loop(0, 3, send_one, 0)

        @pl.when(core == 1)
        def _():
            conv_and_send(0, 0)
            own_half(1).start()
            lax.fori_loop(1, 3, conv_and_send, 0)
            conv_d1(3, 0)

    @pl.when(is_first)
    def _():
        xh[...] = jnp.zeros(xh.shape, BF16)
        hid[0] = jnp.zeros((4, 64, 512), BF16)

    def conv_d0(c):
        with scope("halo_wait"):

            @pl.when(jnp.logical_not(is_first))
            def _():
                if c == 0:
                    lanes = pl.ds(0, 4096)
                    block = xh.at[:, lanes]
                    remote(block, block, halo_sent, halo_sems.at[0], near).wait_recv()
                elif c > 1:
                    halo_copy(c).wait_recv()

        with scope("conv_d0"):
            taps_halo(c)
            first_conv(0, v0, c)

    def finish_d1(c):
        with scope("finish_d1"):
            finish(1, 2, c)

    def send_sums(h, c):
        with scope("across"):
            across(h, c)

    def finish_d0(c):
        with scope("finish_d0"):
            finish(0, 1, c)

    def pass_wb(m):
        with scope("pass_wb"):
            own_half(m).wait_recv()
            pass_on(m)

    def taps2(i, at_i, quarters):
        with scope("taps2"):
            second_taps(i, at_i, quarters)

    to_sibling(wb_send, wb, wb_sent, wb_sems.at[2]).start()
    conv_d0(0)
    conv_d0(1)
    pass_wb(0)
    conv_d0(2)
    pass_wb(1)
    finish_d1(0)
    send_sums(1, 3)
    finish_d1(1)
    send_sums(0, 0)
    conv_d0(3)
    finish_d1(2)
    send_sums(0, 1)
    finish_d1(3)
    send_sums(0, 2)
    load_s2.wait()
    v2[1728:1792] = jnp.zeros((64, QUARTER), BF16)
    taps2(2, 1, range(4))
    finish_d0(0)
    send_sums(0, 3)

    def halo_taps(quarters):
        with scope("hid_wait"):

            @pl.when(jnp.logical_not(is_first))
            def _():
                if len(quarters) == 2:
                    block = hid.at[0, pl.ds(0, 2)]
                    remote(block, block, hid_sent, hid_sems.at[0], near).wait_recv()
                else:
                    hid_copy(quarters[0]).wait_recv()

        taps2(0, 0, quarters)

    halo_taps((0, 1))
    finish_d0(1)
    taps2(1, 2, (0, 1))
    with scope("wait_wb"):
        slots(wb_send, wb, wb_sent, wb_sems.at[2], 2).wait_recv()

    units = ((0, 1), (2,), (3,))

    def unit_lanes(n):
        return pl.ds(128 * units[n][0], 128 * len(units[n]))

    def sib2_copy(n):
        lanes = unit_lanes(n)
        return remote(
            part2.at[1 - core, chip, :, lanes], sib2.at[:, lanes], sib2_sent, z_sems.at[n], near
        )

    def z_copy(n, k):
        lanes = unit_lanes(n)
        return remote(
            z_send.at[k, :, lanes], z_recv.at[core, :, lanes], z_sent, z_sems.at[n],
            (s, (1 - chip) * 2 + k),
        )

    def conv2(n, rows, at):
        lanes = unit_lanes(n)
        sums = jnp.dot(
            wb[:, :, :, at : at + rows].reshape(256, rows),
            v2[at : at + rows, lanes],
            preferred_element_type=F32,
        )
        return sums.reshape(2, 2, 64, 128 * len(units[n]))

    for n, quarters in enumerate(units):
        lanes = unit_lanes(n)
        if n > 0:
            halo_taps((n + 1,))
            if n == 2:
                with scope("conv2_sides"):
                    part2[:, :, :, lanes] = conv2(n, 1152, 0)
            finish_d0(n + 1)
            taps2(1, 2, (n + 1,))
        with scope("conv2"):
            if n == 2:
                part2[:, :, :, lanes] = part2[:, :, :, lanes] + conv2(n, 640, 1152)
            else:
                part2[:, :, :, lanes] = conv2(n, 1792, 0)
            for k in range(2):
                z_send[k, :, lanes] = part2[k, 1 - chip, :, lanes].astype(BF16)
                z_copy(n, k).start()
            sib2_copy(n).start()
    bias_b = column(biases[1])
    for n, quarters in enumerate(units):
        lanes = unit_lanes(n)
        with scope("z_wait"):
            arrived = part2.at[0, :, :, lanes]
            remote(arrived, arrived, z_sent, z_sems.at[n], near).wait_recv()
        far = z_recv[0, :, lanes].astype(F32) + z_recv[1, :, lanes].astype(F32)
        bias = bias_b[:, : 128 * len(quarters)]
        total = part2[core, chip, :, lanes] + sib2[:, lanes] + far + bias
        out[:, lanes] = leaky(total)

    with scope("drain"):
        slots(wa_send, wa, wa_sent, wa_sems.at[1], 2).wait_send()

        @pl.when(core == 0)
        def _():
            slots(wa_send, wa, wa_sent, wa_sems.at[1], 1).wait_send()

        @pl.when(core == 1)
        def _():
            wa_half.wait_send()

        @pl.when(jnp.logical_and(core == 1, passes_down))
        def _():
            wa_half.wait_send()

        @pl.when(jnp.logical_and(core == 1, even_up))
        def _():
            slots(wa_send, wa, wa_sent, wa_sems.at[1], 1).wait_send()

        slots(wb_send, wb, wb_sent, wb_sems.at[2], 2).wait_send()

        @pl.when(passes_down)
        def _():
            slots(wb_send, wb, wb_sent, wb_sems.at[2], 1).wait_send()

        @pl.when(even_up)
        def _():
            slots(wb_send, wb, wb_sent, wb_sems.at[2], 1).wait_send()

        @pl.when(level == 2)
        def _():
            own_half(0).wait_send()

        remote(part.at[:, :, 1 - core], sib, sib_sent, sib_sems.at[0], near).wait_send()
        remote(y_send, y_recv, y_sent, y_sems.at[0, 0], near).wait_send()
        remote(part2.at[1 - core, chip], sib2, sib2_sent, z_sems.at[0], near).wait_send()
        remote(z_send, z_recv, z_sent, z_sems.at[0], near).wait_send()

        @pl.when(jnp.logical_not(is_last))
        def _():
            remote(x.at[pl.ds(96, 32)], xh, halo_sent, halo_sems.at[0], near).wait_send()
            hid_all.wait_send()


def scattered(n_spatial, volume_in, filters_a, bias_a, filters_b, bias_b):
    vmem = pl.BlockSpec(memory_space=pltpu.VMEM)
    hbm = pl.BlockSpec(memory_space=pltpu.HBM)
    dma = pltpu.SemaphoreType.DMA

    def body(*refs):
        kernel(n_spatial, *refs)

    out = pl.pallas_call(
        body,
        out_shape=jax.ShapeDtypeStruct((64, QUARTER), BF16),
        in_specs=[hbm] * 7,
        out_specs=vmem,
        scratch_shapes=[
            pltpu.VMEM((27, 64, 128), BF16),
            pltpu.VMEM((2, 1, 64), BF16),
            pltpu.VMEM((27, 64, 256), BF16),
            pltpu.VMEM((256, 384), BF16),
            pltpu.VMEM((2, 512, 384), BF16),
            pltpu.VMEM((32, 4, ROWS * COLS), BF16),
            pltpu.VMEM((128, ROWS * COLS), BF16),
            pltpu.VMEM((32, ROWS * COLS), BF16),
            pltpu.VMEM((4, 2, 32, 896), BF16),
            pltpu.VMEM((4, 2, 32, 896), BF16),
            pltpu.VMEM((4, 2, 32, 1792), BF16),
            pltpu.VMEM((4, 2, 32, 1792), BF16),
            pltpu.VMEM((896, HALF), BF16),
            pltpu.VMEM((896, HALF), BF16),
            pltpu.VMEM((2, 4, 2, 2, 64, 512), F32),
            pltpu.VMEM((2, 4, 2, 64, 512), F32),
            pltpu.VMEM((2, 4, 64, 512), BF16),
            pltpu.VMEM((2, 4, 64, 512), BF16),
            pltpu.VMEM((3, 4, 64, 512), BF16),
            pltpu.VMEM((1792, QUARTER), BF16),
            pltpu.VMEM((2, 2, 64, 512), F32),
            pltpu.VMEM((64, 512), F32),
            pltpu.VMEM((2, 64, 512), BF16),
            pltpu.VMEM((2, 64, 512), BF16),
            dma((5,)), dma((4,)), dma, dma((3,)), dma((3,)), dma((3,)), dma((6,)), dma((2, 4)), dma((3,)),
            dma((3,)),
        ],
        compiler_params=pltpu.CompilerParams(
            collective_id=0, has_side_effects=True, vmem_limit_bytes=52 * 1024 * 1024
        ),
        name="scattered_convs",
    )(
        *(
            pltpu.with_memory_space_constraint(a, pltpu.HBM)
            for a in (
                volume_in,
                filters_a,
                filters_b,
                bias_a.reshape(1, 64),
                bias_b.reshape(1, 64),
                jnp.asarray(pick_first(), BF16),
                jnp.asarray(pick_second(), BF16),
            )
        )
    )
    return out.reshape(64, 1, QUARTER)


def per_device(volume_in, filters_a, bias_a, filters_b, bias_b):
    n_spatial = lax.axis_size("spatial")
    own = volume_in.shape == (32, 4, ROWS * COLS) and filters_b.shape == (27, 64, 256)
    if own and n_spatial % 8 == 0:
        return scattered(n_spatial, volume_in, filters_a, bias_a, filters_b, bias_b)
    return gathered(volume_in, filters_a, bias_a, filters_b, bias_b)


def solution(mesh):
    in_specs = (
        P("filter", "spatial", None),
        P(None, "filter", None),
        P("filter"),
        P(None, "filter", None),
        P("filter"),
    )
    return jax.shard_map(
        per_device,
        mesh=mesh,
        in_specs=in_specs,
        out_specs=P("filter", "spatial", None),
        check_vma=False,
    )
```
